32 devices in a mesh: grp: 2 (over x), wide: 16 (over z, y, core).
Axes of the slice: x: 2, y: 2, z: 4, core: 2. Of those that a mesh axis runs over, the one named last changes fastest.
Arguments:
- homolog_stack_state: bfloat16 [256, 128, 256], P(('grp', 'wide')), parts along dimension 0, may hold values from -6 to 6
- present_flags: int32 [256, 128], P('grp'), parts along dimension 0, may hold values from 0 to 1, as said below
- chain_ordinal_labels: int32 [256], P('grp'), parts along dimension 0, may hold values from 0 to 383, as said below
- pairwise_repr: bfloat16 [256, 128, 128], P(('grp', 'wide')), parts along dimension 0, may hold values from -6 to 6
- heeding_normalizer_gains: float32 [256], replicated, may hold values from 0.1 to 1.9
- retrieval_weights_qkv: bfloat16 [256, 768], replicated, may hold values from -2.7308912 to 2.7308912
- logistic_weights: bfloat16 [256, 256], replicated, may hold values from -0.375 to 0.375
- logistic_intercept: float32 [256], replicated, may hold values from -4 to 4
- emitted_weights: bfloat16 [256, 256], replicated, may hold values from -0.375 to 0.375
- dyadic_normalizer_gains: float32 [256], replicated, may hold values from 0.1 to 1.9
- former_operand_weights: bfloat16 [256, 32], replicated, may hold values from -0.375 to 0.375
- latter_operand_weights: bfloat16 [256, 32], replicated, may hold values from -0.375 to 0.375
- flattened_outer_projection: bfloat16 [1024, 128], replicated, may hold values from -0.75 to 0.75
- clipped_separation_embedding: bfloat16 [65, 128], replicated, may hold values from -5 to 5
Outputs:
- homolog_changed: bfloat16 [256, 128, 256], P(('grp', 'wide')), parts along dimension 0
- couple_state_changed: bfloat16 [256, 128, 128], P(('grp', 'wide')), parts along dimension 0
The draws below stay inside these ranges and needn't reach their ends.
There are 2 independent parts, one for each index of `grp`. The reference program is written for one: setup_inputs(seed, part) draws one part's arguments, and reference() takes and returns one part's arrays. A program takes and returns all parts, laid end to end along the dimension named above; an argument that names none is the same for every part. Nothing has to cross between parts.
Inputs may be any that keep to these rules, and one draw needn't show every extreme that they name: `present_flags`: every entry of the first sequence is 1. `chain_ordinal_labels`: rises from token to token by 1 to 3.
All inputs are finite; a program needn't handle non-finite values.
Results may differ from the reference program's by a relative error of at most 0.0094.
The reference program's roundings to bfloat16 on the way count: a program that leaves them out, or rounds other values in their place, can miss the bound.
Values may be sent and summed in bfloat16 or wider, within the bound.
No kernel may reach another device: no remote copies, remote signals or barrier semaphores. Data moves between devices by JAX's collectives and lax.ppermute only.
A program may use at most 128 MiB of HBM per device.

```python
import math
import jax
import jax.numpy as jnp
from jax import lax

HOMOLOG_CHANNELS = 256
HEAD_TOTAL = 8
OPERAND_BREADTH = 32
PAIR_WIDTH = 128
RELPOS_CLIP = 32
HOMOLOG_TOTAL = 128
HEAD_SIZE = 32
STRETCH_SIZE = 128


def draw_retrieval_weights_qkv(key, part):
    starting_amount = jnp.clip(jax.random.normal(key, (HOMOLOG_CHANNELS, 3, HOMOLOG_CHANNELS), jnp.float32), -6.0, 6.0)
    starting_amount = starting_amount / math.sqrt(HOMOLOG_CHANNELS)
    return starting_amount.reshape(HOMOLOG_CHANNELS, 3 * HOMOLOG_CHANNELS).astype(jnp.bfloat16)


def draw_present_flags(key, part):
    probe_occurrences = jax.random.fold_in(key, 11)
    probe_element = jax.random.fold_in(key, 12)
    speed_quantities = jax.random.randint(probe_occurrences, (HOMOLOG_TOTAL, 1), 2, 9)
    grid_quantities = jax.random.randint(probe_element, (HOMOLOG_TOTAL, STRETCH_SIZE), 0, 8)
    live = (grid_quantities < speed_quantities).astype(jnp.int32)
    leading_element = (lax.broadcasted_iota(jnp.int32, (HOMOLOG_TOTAL, STRETCH_SIZE), 0) == 0).astype(jnp.int32)
    return jnp.maximum(live, leading_element)


def draw_chain_ordinal_labels(key, part):
    key_step = jax.random.fold_in(key, 21)
    gaps = jax.random.randint(key_step, (STRETCH_SIZE,), 1, 4).astype(jnp.int32)
    running = jnp.cumsum(gaps).astype(jnp.int32)
    after = running[STRETCH_SIZE - 1] - running
    return (3 * STRETCH_SIZE - 1 - after).astype(jnp.int32)


def shard_levels(key, shape, shards, least, largest):
    loudness, own = 1.0, jax.random.fold_in(key, 6)
    for axis_at, blocks in shards:
        draws = jnp.exp(jax.random.uniform(jax.random.fold_in(own, axis_at), (blocks,), jnp.float32, least / len(shards), largest / len(shards)))
        loudness = loudness * jnp.repeat(draws, shape[axis_at] // blocks).reshape([-1 if axis == axis_at else 1 for axis in range(len(shape))])
    return loudness


def noise(stream_key, dims, deviation, bound, cuts=(), held_as=jnp.bfloat16):
    entries = jax.random.normal(stream_key, dims, jnp.float32) * deviation
    if len(cuts) > 0:
        entries = shard_levels(stream_key, dims, cuts, -0.22, 0.18) * entries
    return jnp.clip(entries, min=-bound, max=bound).astype(held_as)


def setup_inputs(seed: int = 0, part: int = 0) -> dict:
    key_of = jax.random.split(jax.random.key(seed), 15)
    own_keys = jax.random.split(jax.random.fold_in(key_of[14], part), 15)
    return {
        "homolog_stack_state": noise(own_keys[0], (HOMOLOG_TOTAL, STRETCH_SIZE, HOMOLOG_CHANNELS), 1.0, 6.0, ((0, 16),)),
        "present_flags": draw_present_flags(jax.random.fold_in(jax.random.fold_in(key_of[14], part), 71), part),
        "chain_ordinal_labels": draw_chain_ordinal_labels(jax.random.fold_in(jax.random.fold_in(key_of[14], part), 71), part),
        "pairwise_repr": noise(own_keys[3], (STRETCH_SIZE, STRETCH_SIZE, PAIR_WIDTH), 1.0, 6.0, ((0, 16),)),
        "heeding_normalizer_gains": jnp.clip(1.0 + 0.18 * jax.random.normal(key_of[4], (HOMOLOG_CHANNELS,), jnp.float32), 0.1, 1.9),
        "retrieval_weights_qkv": draw_retrieval_weights_qkv(jax.random.fold_in(key_of[14], 71), part),
        "logistic_weights": noise(key_of[6], (HOMOLOG_CHANNELS, HOMOLOG_CHANNELS), HOMOLOG_CHANNELS ** -0.5, 0.375),
        "logistic_intercept": noise(key_of[7], (HOMOLOG_CHANNELS,), 1.0, 4.0, (), jnp.float32),
        "emitted_weights": noise(key_of[8], (HOMOLOG_CHANNELS, HOMOLOG_CHANNELS), HOMOLOG_CHANNELS ** -0.5, 0.375),
        "dyadic_normalizer_gains": jnp.clip(1.0 + 0.18 * jax.random.normal(key_of[9], (HOMOLOG_CHANNELS,), jnp.float32), 0.1, 1.9),
        "former_operand_weights": noise(key_of[10], (HOMOLOG_CHANNELS, OPERAND_BREADTH), HOMOLOG_CHANNELS ** -0.5, 0.375),
        "latter_operand_weights": noise(key_of[11], (HOMOLOG_CHANNELS, OPERAND_BREADTH), HOMOLOG_CHANNELS ** -0.5, 0.375),
        "flattened_outer_projection": noise(key_of[12], (OPERAND_BREADTH * OPERAND_BREADTH, PAIR_WIDTH), (2 * OPERAND_BREADTH) ** -0.5, 0.75),
        "clipped_separation_embedding": noise(key_of[13], (2 * RELPOS_CLIP + 1, PAIR_WIDTH), 1.0, 5.0),
    }


epsilon = 1e-05

def standardize_features(values, gain_vector):
    mean = lax.optimization_barrier(jnp.mean(values, axis=-1, keepdims=True))
    centered = values - mean
    variance = lax.optimization_barrier(jnp.mean(centered * centered, axis=-1, keepdims=True))
    return centered * lax.rsqrt(variance + epsilon) * gain_vector.astype(jnp.float32)

def downward_heeding_blend(homolog_stack_state, presence_tally, heeding_normalizer_gains, retrieval_weights_qkv, logistic_weights, logistic_intercept, emitted_weights):
    strand_lines, span_features, feature_count = homolog_stack_state.shape
    standardized_source = standardize_features(homolog_stack_state.astype(jnp.float32), heeding_normalizer_gains).astype(jnp.bfloat16).reshape(strand_lines * span_features, feature_count)
    packed = jnp.dot(standardized_source, retrieval_weights_qkv, preferred_element_type=jnp.float32).astype(jnp.bfloat16)
    packed = packed.reshape(strand_lines, span_features, 3, HEAD_TOTAL, HEAD_SIZE)
    gate = jax.nn.sigmoid(jnp.dot(standardized_source, logistic_weights, preferred_element_type=jnp.float32) + logistic_intercept.astype(jnp.float32))
    gate = gate.reshape(strand_lines, span_features, feature_count)
    queries = packed[:, :, 0].astype(jnp.float32)
    keys = packed[:, :, 1].astype(jnp.float32)
    values = packed[:, :, 2].astype(jnp.float32)
    logits = jnp.einsum('sthd,uthd->thsu', queries, keys) / math.sqrt(HEAD_SIZE)
    logits = logits + 1000000000.0 * (presence_tally.T[:, None, None, :] - 1.0)
    attn_weights = jax.nn.softmax(logits, axis=-1).astype(jnp.bfloat16)
    mixed = jnp.einsum('thsu,uthd->sthd', attn_weights.astype(jnp.float32), values).reshape(strand_lines, span_features, feature_count)
    gated = (mixed * gate).astype(jnp.bfloat16).reshape(strand_lines * span_features, feature_count)
    increment_terms = jnp.dot(gated, emitted_weights, preferred_element_type=jnp.float32).reshape(strand_lines, span_features, feature_count)
    return (homolog_stack_state.astype(jnp.float32) + increment_terms).astype(jnp.bfloat16)

def map_operand_half(alignment_fresh, presence_tally, gain_vector, weight_matrix):
    strand_lines, span_features, feature_count = alignment_fresh.shape
    standardized_source = standardize_features(alignment_fresh.astype(jnp.float32), gain_vector).astype(jnp.bfloat16).reshape(strand_lines * span_features, feature_count)
    factor = jnp.dot(standardized_source, weight_matrix, preferred_element_type=jnp.float32).reshape(strand_lines, span_features, weight_matrix.shape[1])
    return (factor * presence_tally[:, :, None]).astype(jnp.bfloat16)

def reference(homolog_stack_state, present_flags, chain_ordinal_labels, pairwise_repr, heeding_normalizer_gains, retrieval_weights_qkv, logistic_weights, logistic_intercept, emitted_weights, dyadic_normalizer_gains, former_operand_weights, latter_operand_weights, flattened_outer_projection, clipped_separation_embedding):
    existence_overall = present_flags.astype(jnp.float32)
    homolog_changed = downward_heeding_blend(homolog_stack_state, existence_overall, heeding_normalizer_gains, retrieval_weights_qkv, logistic_weights, logistic_intercept, emitted_weights)
    former_operand = map_operand_half(homolog_changed, existence_overall, dyadic_normalizer_gains, former_operand_weights)
    latter_operand = map_operand_half(homolog_changed, existence_overall, dyadic_normalizer_gains, latter_operand_weights)
    block = math.gcd(STRETCH_SIZE, 64)
    span = 2 * RELPOS_CLIP + 1

    def pair_block(start):
        left_block = lax.dynamic_slice_in_dim(former_operand, start, block, 1)
        outer = jnp.einsum('sic,sje->ijce', left_block.astype(jnp.float32), latter_operand.astype(jnp.float32))
        outer = outer.astype(jnp.bfloat16).reshape(block * STRETCH_SIZE, OPERAND_BREADTH * OPERAND_BREADTH)
        projected = jnp.dot(outer, flattened_outer_projection, preferred_element_type=jnp.float32).reshape(block, STRETCH_SIZE, PAIR_WIDTH)
        mask_block = lax.dynamic_slice_in_dim(existence_overall, start, block, 1)
        counts = jnp.dot(mask_block.T, existence_overall, precision=lax.Precision.HIGHEST)
        residue_block = lax.dynamic_slice_in_dim(chain_ordinal_labels, start, block, 0)
        offsets = jnp.clip(residue_block[:, None] - chain_ordinal_labels[None, :], -RELPOS_CLIP, RELPOS_CLIP) + RELPOS_CLIP
        one_hot = (offsets[:, :, None] == jnp.arange(span, dtype=jnp.int32)[None, None, :]).astype(jnp.bfloat16)
        relpos = jnp.dot(one_hot.reshape(block * STRETCH_SIZE, span), clipped_separation_embedding, preferred_element_type=jnp.float32)
        relpos = relpos.reshape(block, STRETCH_SIZE, PAIR_WIDTH)
        starting_amount = lax.dynamic_slice_in_dim(pairwise_repr, start, block, 0).astype(jnp.float32)
        return (starting_amount + relpos + projected / counts[:, :, None]).astype(jnp.bfloat16)
    starts = jnp.arange(STRETCH_SIZE // block, dtype=jnp.int32) * block
    blocks = lax.map(pair_block, starts)
    couple_state_changed = blocks.reshape(STRETCH_SIZE, STRETCH_SIZE, PAIR_WIDTH)
    return (homolog_changed, couple_state_changed)
```

```python
import functools
import math

import jax
import jax.numpy as jnp
from jax import lax
from jax.experimental import pallas as pl
from jax.experimental.pallas import tpu as pltpu
from jax.sharding import PartitionSpec as P

HEAD_TOTAL = 8
RELPOS_CLIP = 32
HEAD_SIZE = 32
EPSILON = 1e-05
LANES = 128
F32 = jnp.float32
BF16 = jnp.bfloat16


NT = (((1,), (1,)), ((), ()))
TN = (((0,), (0,)), ((), ()))


def standardize(values, gain_row):
    mean = jnp.mean(values, axis=-1, keepdims=True)
    centered = values - mean
    variance = jnp.mean(centered * centered, axis=-1, keepdims=True)
    return centered * lax.rsqrt(variance + EPSILON) * gain_row


def put_rows(ref, rows, values):
    for part in range(ref.shape[0]):
        ref[part, rows, :] = values[:, part * LANES : (part + 1) * LANES]


def take_rows(ref, rows):
    return jnp.concatenate([ref[part, rows, :] for part in range(ref.shape[0])], axis=1)


def attention_kernel(
    tokens,
    x_ref,
    bias_ref,
    flag_ref,
    gain1_ref,
    wqvg_ref,
    wk_ref,
    intercept_ref,
    wo_ref,
    gain2_ref,
    wlr_ref,
    hc_ref,
    left_ref,
    right_ref,
    xf_ref,
    normed_ref,
    hcf_ref,
    rf_ref,
):
    rows, channels = x_ref.shape
    seqs = rows // tokens
    breadth = wlr_ref.shape[0] // 2
    group_heads = LANES // HEAD_SIZE

    chunk = min(rows, 256)

    @pl.loop(0, rows // chunk)
    def _(at):
        here = pl.ds(pl.multiple_of(at * chunk, chunk), chunk)
        values = x_ref[here, :].astype(F32)
        put_rows(xf_ref, here, values)
        put_rows(normed_ref, here, standardize(values, gain1_ref[...]))

    head_of_lane = lax.broadcasted_iota(jnp.int32, (seqs, LANES), 1) // HEAD_SIZE

    @pl.loop(0, tokens)
    def _(t):
        mine = pl.ds(t, seqs, stride=tokens)
        normed = take_rows(normed_ref, mine).astype(BF16)
        qvg = lax.dot_general(wqvg_ref[...], normed, NT, preferred_element_type=F32)
        keys = jnp.dot(normed, wk_ref[...], preferred_element_type=F32).astype(BF16)
        queries_t = qvg[:channels].astype(BF16)
        values_t = qvg[channels : 2 * channels].astype(BF16)
        gate_t = jax.nn.sigmoid(qvg[2 * channels :] + intercept_ref[...])
        bias = bias_ref[t]
        mixed = []
        for g in range(channels // LANES):
            span = slice(g * LANES, (g + 1) * LANES)
            keys_g = keys[:, span]
            masked = jnp.concatenate(
                [
                    jnp.where(head_of_lane == h, keys_g, jnp.zeros_like(keys_g))
                    for h in range(group_heads)
                ],
                axis=0,
            )
            logits_g = jnp.dot(masked, queries_t[span], preferred_element_type=F32)
            for h in range(group_heads):
                logits = logits_g[h * seqs : (h + 1) * seqs] * (1.0 / math.sqrt(HEAD_SIZE)) + bias
                powers = jnp.exp(logits - jnp.max(logits, axis=0, keepdims=True))
                share = 1.0 / jnp.sum(powers, axis=0, keepdims=True)
                weights = (powers * share).astype(BF16)
                first = g * LANES + h * HEAD_SIZE
                mixed.append(
                    jnp.dot(
                        values_t[first : first + HEAD_SIZE], weights, preferred_element_type=F32
                    )
                )
        gated = (jnp.concatenate(mixed, axis=0) * gate_t).astype(BF16)
        delta = lax.dot_general(gated, wo_ref[...], TN, preferred_element_type=F32)
        changed = (take_rows(xf_ref, mine) + delta).astype(BF16).astype(F32)
        put_rows(hcf_ref, mine, changed)
        normed2 = standardize(changed, gain2_ref[...]).astype(BF16)
        factors = lax.dot_general(wlr_ref[...], normed2, NT, preferred_element_type=F32)
        factors = factors * flag_ref[t]
        left_ref[t] = factors[:breadth].astype(BF16)
        rf_ref[pl.ds(t, breadth, stride=tokens), :] = factors[breadth:]

    hc_ref[...] = take_rows(hcf_ref, slice(None)).astype(BF16)
    right_ref[...] = rf_ref[...].astype(BF16)


def attention(x_rows, bias, flag_rows, gain1, wqvg, wk, intercept, wo, gain2, wlr, tokens):
    rows, channels = x_rows.shape
    seqs = rows // tokens
    breadth = wlr.shape[0] // 2
    vmem = pl.BlockSpec(memory_space=pltpu.VMEM)
    return pl.pallas_call(
        functools.partial(attention_kernel, tokens),
        out_shape=(
            jax.ShapeDtypeStruct((rows, channels), BF16),
            jax.ShapeDtypeStruct((tokens, breadth, seqs), BF16),
            jax.ShapeDtypeStruct((breadth * tokens, seqs), BF16),
        ),
        in_specs=[vmem] * 10,
        out_specs=(vmem, vmem, vmem),
        scratch_shapes=[
            pltpu.VMEM((channels // LANES, rows, LANES), F32),
            pltpu.VMEM((channels // LANES, rows, LANES), F32),
            pltpu.VMEM((channels // LANES, rows, LANES), F32),
            pltpu.VMEM((breadth * tokens, seqs), F32),
        ],
        cost_estimate=pl.CostEstimate(
            flops=2 * rows * channels * (6 * channels), bytes_accessed=4 * rows * channels, transcendentals=0
        ),
        name="attention",
    )(x_rows, bias, flag_rows, gain1, wqvg, wk, intercept, wo, gain2, wlr)


def slot_of(block, stages):
    slot = 0
    for stride, size in reversed(stages):
        slot = slot * size + (block // stride) % size
    return slot


def pair_kernel(
    stages, per_device, me_ref, left_ref, right_ref, weight_ref, share_ref, base_ref, out_ref, outer_ref
):
    tok_local, breadth, seqs = left_ref.shape
    width = out_ref.shape[1]
    here = pl.program_id(0)
    devices_here = width // per_device
    me = me_ref[0]
    left = left_ref[...].reshape(tok_local * breadth, seqs)
    slots = [
        slot_of(jnp.bitwise_xor(me, here * devices_here + b), stages) for b in range(devices_here)
    ]

    for e in range(breadth):
        right = jnp.concatenate(
            [right_ref[slot, e * per_device : (e + 1) * per_device, :] for slot in slots], axis=0
        )
        outer = lax.dot_general(left, right, NT, preferred_element_type=F32).astype(BF16)
        outer_ref[:, e * breadth : (e + 1) * breadth, :] = outer.reshape(tok_local, breadth, width)

    for i in range(tok_local):
        projected = jnp.dot(weight_ref[...], outer_ref[i], preferred_element_type=F32)
        projected = projected * share_ref[i : i + 1, :]
        out_ref[i] = (base_ref[i] + projected.T).astype(BF16)


def pair_update(me, left, right_all, weight_t, share, base, stages):
    tok_local, breadth, seqs = left.shape
    pair_width = weight_t.shape[0]
    per_device = right_all.shape[1] // breadth
    columns = base.shape[1]
    width = min(columns, LANES)
    return pl.pallas_call(
        functools.partial(pair_kernel, stages, per_device),
        grid_spec=pltpu.PrefetchScalarGridSpec(
            num_scalar_prefetch=1,
            grid=(columns // width,),
            in_specs=[
                pl.BlockSpec(left.shape, lambda j, me: (0, 0, 0)),
                pl.BlockSpec(right_all.shape, lambda j, me: (0, 0, 0)),
                pl.BlockSpec(weight_t.shape, lambda j, me: (0, 0)),
                pl.BlockSpec((tok_local, width), lambda j, me: (0, j)),
                pl.BlockSpec((tok_local, width, pair_width), lambda j, me: (0, j, 0)),
            ],
            out_specs=pl.BlockSpec((tok_local, width, pair_width), lambda j, me: (0, j, 0)),
            scratch_shapes=[pltpu.VMEM((tok_local, breadth * breadth, width), BF16)],
        ),
        out_shape=jax.ShapeDtypeStruct(base.shape, BF16),
        cost_estimate=pl.CostEstimate(
            flops=2 * tok_local * columns * breadth * breadth * (seqs + pair_width),
            bytes_accessed=8 * tok_local * columns * pair_width,
            transcendentals=0,
        ),
        name="pair_update",
    )(me, left, right_all, weight_t, share, base)


def gather_stages(size):
    chips = size // 2
    high = 2 ** math.ceil(math.log2(chips) / 2)
    low = chips // high
    return [(2 * low, high), (2, low), (1, 2)]


def gather_blocks(block, size, stages):
    held = block[None]
    for stride, members in stages:
        parts = [held]
        for k in range(1, members):
            pairs = [(d, d ^ (k * stride)) for d in range(size)]
            parts.append(lax.ppermute(held, "wide", pairs))
        held = jnp.concatenate(parts, axis=0)
    return held


def on_device(
    size,
    homolog_stack_state,
    present_flags,
    chain_ordinal_labels,
    pairwise_repr,
    heeding_normalizer_gains,
    retrieval_weights_qkv,
    logistic_weights,
    logistic_intercept,
    emitted_weights,
    dyadic_normalizer_gains,
    former_operand_weights,
    latter_operand_weights,
    flattened_outer_projection,
    clipped_separation_embedding,
):
    me = lax.axis_index("wide")
    seq_local, columns, channels = homolog_stack_state.shape
    tok_local = pairwise_repr.shape[0]
    seqs = seq_local * size
    breadth = former_operand_weights.shape[1]
    pair_width = flattened_outer_projection.shape[1]
    stages = gather_stages(size)

    sent = homolog_stack_state.reshape(seq_local, size, tok_local, channels).transpose(1, 0, 2, 3)
    x_rows = lax.all_to_all(sent, "wide", 0, 0, tiled=True).reshape(seqs * tok_local, channels)

    flags = present_flags.astype(F32)
    mine = lax.dynamic_slice_in_dim(flags, me * tok_local, tok_local, 1)
    flag_rows = mine.T[:, None, :]
    bias = jnp.broadcast_to((1000000000.0 * (mine.T - 1.0))[:, :, None], (tok_local, seqs, seqs))
    weights_t = retrieval_weights_qkv.T
    wqvg = jnp.concatenate(
        [weights_t[:channels], weights_t[2 * channels :], logistic_weights.T], axis=0
    )
    wk = retrieval_weights_qkv[:, channels : 2 * channels]
    wlr = jnp.concatenate([former_operand_weights.T, latter_operand_weights.T], axis=0)
    projection_t = (
        flattened_outer_projection.reshape(breadth, breadth, pair_width)
        .transpose(2, 1, 0)
        .reshape(pair_width, breadth * breadth)
    )
    counts = jnp.dot(mine.T, flags, precision=lax.Precision.HIGHEST)
    share = 1.0 / counts
    labels_mine = lax.dynamic_slice_in_dim(chain_ordinal_labels, me * tok_local, tok_local, 0)
    offsets = (
        jnp.clip(labels_mine[:, None] - chain_ordinal_labels[None, :], -RELPOS_CLIP, RELPOS_CLIP)
        + RELPOS_CLIP
    )
    span = clipped_separation_embedding.shape[0]
    one_hot = (offsets[:, :, None] == jnp.arange(span, dtype=jnp.int32)[None, None, :]).astype(BF16)
    relpos = jnp.dot(
        one_hot.reshape(tok_local * columns, span),
        clipped_separation_embedding,
        preferred_element_type=F32,
    ).reshape(tok_local, columns, pair_width)
    base = pairwise_repr.astype(F32) + relpos

    changed_rows, left, right = attention(
        x_rows,
        bias,
        flag_rows,
        heeding_normalizer_gains[None, :],
        wqvg,
        wk,
        logistic_intercept[:, None],
        emitted_weights,
        dyadic_normalizer_gains[None, :],
        wlr,
        tok_local,
    )

    right_all = gather_blocks(right, size, stages)
    back = lax.all_to_all(
        changed_rows.reshape(size, seq_local, tok_local, channels), "wide", 0, 0, tiled=True
    )
    homolog_changed = back.transpose(1, 0, 2, 3).reshape(seq_local, columns, channels)
    couple_state_changed = pair_update(
        me.reshape(1), left, right_all, projection_t, share, base, stages
    )
    return (homolog_changed, couple_state_changed)


def solution(mesh):
    in_specs = (
        P(("grp", "wide"), None, None),
        P("grp", None),
        P("grp"),
        P(("grp", "wide"), None, None),
    ) + (P(),) * 10
    out_specs = (P(("grp", "wide"), None, None), P(("grp", "wide"), None, None))
    return jax.shard_map(
        functools.partial(on_device, mesh.shape["wide"]),
        mesh=mesh,
        in_specs=in_specs,
        out_specs=out_specs,
        check_vma=False,
    )
```

```python
import functools
import math

import jax
import jax.numpy as jnp
from jax import lax
from jax.experimental import pallas as pl
from jax.experimental.pallas import tpu as pltpu
from jax.sharding import PartitionSpec as P

HEAD_TOTAL = 8
RELPOS_CLIP = 32
HEAD_SIZE = 32
EPSILON = 1e-05
LANES = 128
F32 = jnp.float32
BF16 = jnp.bfloat16


NT = (((1,), (1,)), ((), ()))
TN = (((0,), (0,)), ((), ()))


def standardize(values, gain_row):
    mean = jnp.mean(values, axis=-1, keepdims=True)
    centered = values - mean
    variance = jnp.mean(centered * centered, axis=-1, keepdims=True)
    return centered * lax.rsqrt(variance + EPSILON) * gain_row


def put_rows(ref, rows, values):
    for part in range(ref.shape[0]):
        ref[part, rows, :] = values[:, part * LANES : (part + 1) * LANES]


def take_rows(ref, rows):
    return jnp.concatenate([ref[part, rows, :] for part in range(ref.shape[0])], axis=1)


def attention_kernel(
    tokens,
    paired,
    x_ref,
    flag_ref,
    gain1_ref,
    wqvg_ref,
    wk_ref,
    intercept_ref,
    wo_ref,
    gain2_ref,
    wlr_ref,
    hc_ref,
    left_ref,
    right_ref,
    xf_ref,
    normed_ref,
    hcf_ref,
    rf_ref,
    queries_ref,
    keys_ref,
    values_ref,
    gate_ref,
    gated_ref,
):
    rows, channels = x_ref.shape
    seqs = rows // tokens
    breadth = wlr_ref.shape[0] // 2
    group_heads = LANES // HEAD_SIZE
    scale = math.log2(math.e) / math.sqrt(HEAD_SIZE)
    hidden = 1000000000.0 * math.log2(math.e)

    chunk = min(rows, 256)

    @pl.loop(0, rows // chunk)
    def _(at):
        here = pl.ds(pl.multiple_of(at * chunk, chunk), chunk)
        values = x_ref[here, :].astype(F32)
        put_rows(xf_ref, here, values)
        put_rows(normed_ref, here, standardize(values, gain1_ref[...]))

    def rows_of(ref, pair):
        return jnp.concatenate(
            [
                take_rows(ref, pl.ds(pair * paired + k, seqs, stride=tokens))
                for k in range(paired)
            ],
            axis=0,
        )

    @pl.loop(0, tokens // paired)
    def _(pair):
        normed = rows_of(normed_ref, pair).astype(BF16)
        qvg = lax.dot_general(wqvg_ref[...], normed, NT, preferred_element_type=F32)
        keys_ref[pair] = jnp.dot(normed, wk_ref[...], preferred_element_type=F32).astype(BF16)
        queries_ref[pair] = qvg[:channels].astype(BF16)
        values_ref[pair] = qvg[channels : 2 * channels].astype(BF16)
        gate_ref[pair] = 0.5 * jnp.tanh(0.5 * (qvg[2 * channels :] + intercept_ref[...])) + 0.5

    head_of_lane = lax.broadcasted_iota(jnp.int32, (seqs, LANES), 1) // HEAD_SIZE

    @pl.loop(0, tokens // paired)
    def _(pair):
        for k in range(paired):
            at = slice(k * seqs, (k + 1) * seqs)
            flags = flag_ref[pair * paired + k]
            bias = jnp.broadcast_to((hidden * (flags - 1.0)).T, (seqs, seqs))
            for g in range(channels // LANES):
                span = slice(g * LANES, (g + 1) * LANES)
                keys_g = keys_ref[pair, at, span]
                masked = jnp.concatenate(
                    [
                        jnp.where(head_of_lane == h, keys_g, jnp.zeros_like(keys_g))
                        for h in range(group_heads)
                    ],
                    axis=0,
                )
                logits_g = jnp.dot(
                    masked, queries_ref[pair, span, at], preferred_element_type=F32
                )
                for h in range(group_heads):
                    logits = logits_g[h * seqs : (h + 1) * seqs] * scale + bias
                    powers = jnp.exp2(logits - jnp.max(logits, axis=0, keepdims=True))
                    share = 1.0 / jnp.sum(powers, axis=0, keepdims=True)
                    weights = (powers * share).astype(BF16)
                    head = slice(g * LANES + h * HEAD_SIZE, g * LANES + (h + 1) * HEAD_SIZE)
                    mixed = jnp.dot(
                        values_ref[pair, head, at], weights, preferred_element_type=F32
                    )
                    gated_ref[pair, head, at] = (mixed * gate_ref[pair, head, at]).astype(BF16)

    @pl.loop(0, tokens // paired)
    def _(pair):
        delta = lax.dot_general(gated_ref[pair], wo_ref[...], TN, preferred_element_type=F32)
        changed = (rows_of(xf_ref, pair) + delta).astype(BF16).astype(F32)
        normed2 = standardize(changed, gain2_ref[...]).astype(BF16)
        factors = lax.dot_general(wlr_ref[...], normed2, NT, preferred_element_type=F32)
        for k in range(paired):
            t = pair * paired + k
            at = slice(k * seqs, (k + 1) * seqs)
            put_rows(hcf_ref, pl.ds(t, seqs, stride=tokens), changed[at])
            mine = factors[:, at] * flag_ref[t]
            left_ref[t] = mine[:breadth].astype(BF16)
            rf_ref[pl.ds(t, breadth, stride=tokens), :] = mine[breadth:]

    hc_ref[...] = take_rows(hcf_ref, slice(None)).astype(BF16)
    right_ref[...] = rf_ref[...].astype(BF16)


def attention(x_rows, flag_rows, gain1, wqvg, wk, intercept, wo, gain2, wlr, tokens):
    rows, channels = x_rows.shape
    seqs = rows // tokens
    breadth = wlr.shape[0] // 2
    paired = 2 if tokens % 2 == 0 else 1
    pairs, lanes = tokens // paired, paired * seqs
    slab = pltpu.VMEM((channels // LANES, rows, LANES), F32)
    vmem = pl.BlockSpec(memory_space=pltpu.VMEM)
    return pl.pallas_call(
        functools.partial(attention_kernel, tokens, paired),
        out_shape=(
            jax.ShapeDtypeStruct((rows, channels), BF16),
            jax.ShapeDtypeStruct((tokens, breadth, seqs), BF16),
            jax.ShapeDtypeStruct((breadth * tokens, seqs), BF16),
        ),
        in_specs=[vmem] * 9,
        out_specs=(vmem, vmem, vmem),
        scratch_shapes=[
            slab,
            slab,
            slab,
            pltpu.VMEM((breadth * tokens, seqs), F32),
            pltpu.VMEM((pairs, channels, lanes), BF16),
            pltpu.VMEM((pairs, lanes, channels), BF16),
            pltpu.VMEM((pairs, channels, lanes), BF16),
            pltpu.VMEM((pairs, channels, lanes), F32),
            pltpu.VMEM((pairs, channels, lanes), BF16),
        ],
        compiler_params=pltpu.CompilerParams(vmem_limit_bytes=24 * 2**20),
        cost_estimate=pl.CostEstimate(
            flops=2 * rows * channels * (6 * channels),
            bytes_accessed=4 * rows * channels,
            transcendentals=0,
        ),
        name="attention",
    )(x_rows, flag_rows, gain1, wqvg, wk, intercept, wo, gain2, wlr)


def slot_of(block, stages):
    slot = 0
    for stride, size in reversed(stages):
        slot = slot * size + (block // stride) % size
    return slot


def pair_kernel(
    stages, per_device, me_ref, left_ref, right_ref, weight_ref, share_ref, base_ref, out_ref, outer_ref
):
    tok_local, breadth, seqs = left_ref.shape
    width = out_ref.shape[1]
    here = pl.program_id(0)
    devices_here = width // per_device
    me = me_ref[0]
    left = left_ref[...].reshape(tok_local * breadth, seqs)
    slots = [
        slot_of(jnp.bitwise_xor(me, here * devices_here + b), stages) for b in range(devices_here)
    ]

    for e in range(breadth):
        right = jnp.concatenate(
            [right_ref[slot, e * per_device : (e + 1) * per_device, :] for slot in slots], axis=0
        )
        outer = lax.dot_general(left, right, NT, preferred_element_type=F32).astype(BF16)
        outer_ref[:, e * breadth : (e + 1) * breadth, :] = outer.reshape(tok_local, breadth, width)

    for i in range(tok_local):
        projected = jnp.dot(weight_ref[...], outer_ref[i], preferred_element_type=F32)
        projected = projected * share_ref[i : i + 1, :]
        out_ref[i] = (base_ref[i] + projected.T).astype(BF16)


def pair_update(me, left, right_all, weight_t, share, base, stages):
    tok_local, breadth, seqs = left.shape
    pair_width = weight_t.shape[0]
    per_device = right_all.shape[1] // breadth
    columns = base.shape[1]
    width = min(columns, LANES)
    return pl.pallas_call(
        functools.partial(pair_kernel, stages, per_device),
        grid_spec=pltpu.PrefetchScalarGridSpec(
            num_scalar_prefetch=1,
            grid=(columns // width,),
            in_specs=[
                pl.BlockSpec(left.shape, lambda j, me: (0, 0, 0)),
                pl.BlockSpec(right_all.shape, lambda j, me: (0, 0, 0)),
                pl.BlockSpec(weight_t.shape, lambda j, me: (0, 0)),
                pl.BlockSpec((tok_local, width), lambda j, me: (0, j)),
                pl.BlockSpec((tok_local, width, pair_width), lambda j, me: (0, j, 0)),
            ],
            out_specs=pl.BlockSpec((tok_local, width, pair_width), lambda j, me: (0, j, 0)),
            scratch_shapes=[pltpu.VMEM((tok_local, breadth * breadth, width), BF16)],
        ),
        out_shape=jax.ShapeDtypeStruct(base.shape, BF16),
        compiler_params=pltpu.CompilerParams(vmem_limit_bytes=24 * 2**20),
        cost_estimate=pl.CostEstimate(
            flops=2 * tok_local * columns * breadth * breadth * (seqs + pair_width),
            bytes_accessed=8 * tok_local * columns * pair_width,
            transcendentals=0,
        ),
        name="pair_update",
    )(me, left, right_all, weight_t, share, base)


def gather_stages(size):
    chips = size // 2
    high = 2 ** math.ceil(math.log2(chips) / 2)
    low = chips // high
    return [(2 * low, high), (2, low), (1, 2)]


def gather_blocks(block, size, stages):
    held = block[None]
    for stride, members in stages:
        parts = [held]
        for k in range(1, members):
            pairs = [(d, d ^ (k * stride)) for d in range(size)]
            parts.append(lax.ppermute(held, "wide", pairs))
        held = jnp.concatenate(parts, axis=0)
    return held


def on_device(
    size,
    homolog_stack_state,
    present_flags,
    chain_ordinal_labels,
    pairwise_repr,
    heeding_normalizer_gains,
    retrieval_weights_qkv,
    logistic_weights,
    logistic_intercept,
    emitted_weights,
    dyadic_normalizer_gains,
    former_operand_weights,
    latter_operand_weights,
    flattened_outer_projection,
    clipped_separation_embedding,
):
    me = lax.axis_index("wide")
    seq_local, columns, channels = homolog_stack_state.shape
    tok_local = pairwise_repr.shape[0]
    seqs = seq_local * size
    breadth = former_operand_weights.shape[1]
    pair_width = flattened_outer_projection.shape[1]
    stages = gather_stages(size)

    sent = homolog_stack_state.reshape(seq_local, size, tok_local, channels).transpose(1, 0, 2, 3)
    x_rows = lax.all_to_all(sent, "wide", 0, 0, tiled=True).reshape(seqs * tok_local, channels)

    flags = present_flags.astype(F32)
    mine = lax.dynamic_slice_in_dim(flags, me * tok_local, tok_local, 1)
    flag_rows = mine.T[:, None, :]
    weights_t = retrieval_weights_qkv.T
    wqvg = jnp.concatenate(
        [weights_t[:channels], weights_t[2 * channels :], logistic_weights.T], axis=0
    )
    wk = retrieval_weights_qkv[:, channels : 2 * channels]
    wlr = jnp.concatenate([former_operand_weights.T, latter_operand_weights.T], axis=0)
    projection_t = (
        flattened_outer_projection.reshape(breadth, breadth, pair_width)
        .transpose(2, 1, 0)
        .reshape(pair_width, breadth * breadth)
    )
    counts = jnp.dot(mine.T, flags, precision=lax.Precision.HIGHEST)
    share = 1.0 / counts
    labels_mine = lax.dynamic_slice_in_dim(chain_ordinal_labels, me * tok_local, tok_local, 0)
    offsets = (
        jnp.clip(labels_mine[:, None] - chain_ordinal_labels[None, :], -RELPOS_CLIP, RELPOS_CLIP)
        + RELPOS_CLIP
    )
    span = clipped_separation_embedding.shape[0]
    one_hot = (offsets[:, :, None] == jnp.arange(span, dtype=jnp.int32)[None, None, :]).astype(BF16)
    relpos = jnp.dot(
        one_hot.reshape(tok_local * columns, span),
        clipped_separation_embedding,
        preferred_element_type=F32,
    ).reshape(tok_local, columns, pair_width)
    base = pairwise_repr.astype(F32) + relpos

    x_rows, base, share, projection_t = lax.optimization_barrier(
        (x_rows, base, share, projection_t)
    )

    changed_rows, left, right = attention(
        x_rows,
        flag_rows,
        heeding_normalizer_gains[None, :],
        wqvg,
        wk,
        logistic_intercept[:, None],
        emitted_weights,
        dyadic_normalizer_gains[None, :],
        wlr,
        tok_local,
    )

    right_all = gather_blocks(right, size, stages)
    back = lax.all_to_all(
        changed_rows.reshape(size, seq_local, tok_local, channels), "wide", 0, 0, tiled=True
    )
    homolog_changed = back.transpose(1, 0, 2, 3).reshape(seq_local, columns, channels)
    couple_state_changed = pair_update(
        me.reshape(1), left, right_all, projection_t, share, base, stages
    )
    return (homolog_changed, couple_state_changed)


def solution(mesh):
    in_specs = (
        P(("grp", "wide"), None, None),
        P("grp", None),
        P("grp"),
        P(("grp", "wide"), None, None),
    ) + (P(),) * 10
    out_specs = (P(("grp", "wide"), None, None), P(("grp", "wide"), None, None))
    return jax.shard_map(
        functools.partial(on_device, mesh.shape["wide"]),
        mesh=mesh,
        in_specs=in_specs,
        out_specs=out_specs,
        check_vma=False,
    )
```

```python
import functools
import math

import jax
import jax.numpy as jnp
from jax import lax
from jax.experimental import pallas as pl
from jax.experimental.pallas import tpu as pltpu
from jax.sharding import PartitionSpec as P

HEAD_TOTAL = 8
RELPOS_CLIP = 32
HEAD_SIZE = 32
EPSILON = 1e-05
LANES = 128
F32 = jnp.float32
BF16 = jnp.bfloat16


NT = (((1,), (1,)), ((), ()))
TN = (((0,), (0,)), ((), ()))


def standardize(values, gain_row):
    mean = jnp.mean(values, axis=-1, keepdims=True)
    centered = values - mean
    variance = jnp.mean(centered * centered, axis=-1, keepdims=True)
    return centered * lax.rsqrt(variance + EPSILON) * gain_row


def put_rows(ref, rows, values):
    for part in range(ref.shape[0]):
        ref[part, rows, :] = values[:, part * LANES : (part + 1) * LANES]


def take_rows(ref, rows):
    return jnp.concatenate([ref[part, rows, :] for part in range(ref.shape[0])], axis=1)


def attention_kernel(
    tokens,
    x_ref,
    bias_ref,
    flag_ref,
    gains_ref,
    wqvg_ref,
    wk_ref,
    intercept_ref,
    wo_ref,
    wlr_ref,
    hc_ref,
    left_ref,
    right_ref,
    xf_ref,
    normed_ref,
    hcf_ref,
    rf_ref,
    queries_ref,
    keys_ref,
    values_ref,
    gate_ref,
    gated_ref,
    *group_refs,
):
    logits_refs, weights_refs = group_refs[::2], group_refs[1::2]
    rows, channels = x_ref.shape
    seqs = rows // tokens
    breadth = wlr_ref.shape[0] // 2
    group_heads = LANES // HEAD_SIZE
    scale = math.log2(math.e) / math.sqrt(HEAD_SIZE)

    values = x_ref[...].astype(F32)
    put_rows(xf_ref, slice(None), values)
    put_rows(normed_ref, slice(None), standardize(values, gains_ref[0:1, :]))

    def rows_of(ref, t):
        return take_rows(ref, pl.ds(t, seqs, stride=tokens))

    normed = jnp.concatenate([rows_of(normed_ref, t) for t in range(tokens)], axis=0).astype(BF16)
    qvg = lax.dot_general(wqvg_ref[...], normed, NT, preferred_element_type=F32)
    keys = jnp.dot(normed, wk_ref[...], preferred_element_type=F32).astype(BF16)
    gate = 0.5 * jnp.tanh(0.5 * (qvg[2 * channels :] + intercept_ref[...])) + 0.5
    for t in range(tokens):
        at = slice(t * seqs, (t + 1) * seqs)
        queries_ref[t] = qvg[:channels, at].astype(BF16)
        values_ref[t] = qvg[channels : 2 * channels, at].astype(BF16)
        gate_ref[t] = gate[:, at]
        keys_ref[t] = keys[at]

    groups = channels // LANES

    def score(t, held):
        token_row = lax.broadcasted_iota(jnp.int32, (LANES, seqs), 0) == t
        token_row = jnp.where(token_row, 1.0, 0.0).astype(BF16)
        for g in range(groups):
            keys_g = jnp.concatenate(
                [keys_ref[t, :, g * LANES : (g + 1) * LANES], bias_ref[...]], axis=1
            )
            columns = []
            for h in range(group_heads):
                first = g * LANES + h * HEAD_SIZE
                parts = [queries_ref[t, first : first + HEAD_SIZE], token_row]
                above, below = h * HEAD_SIZE, LANES - (h + 1) * HEAD_SIZE
                if below:
                    parts.insert(1, jnp.zeros((below, seqs), BF16))
                if above:
                    parts.insert(0, jnp.zeros((above, seqs), BF16))
                columns.append(jnp.concatenate(parts, axis=0))
            logits_refs[held][g] = jnp.dot(
                keys_g, jnp.concatenate(columns, axis=1), preferred_element_type=F32
            )

    def weigh(held):
        for g in range(groups):
            for h in range(group_heads):
                head = slice(h * seqs, (h + 1) * seqs)
                logits = logits_refs[held][g, :, head]
                highest = jnp.max(logits, axis=0, keepdims=True)
                powers = jnp.exp2((logits - highest) * scale)
                share = 1.0 / jnp.sum(powers, axis=0, keepdims=True)
                weights_refs[held][g, :, head] = (powers * share).astype(BF16)

    def mix(t, held):
        for g in range(groups):
            for h in range(group_heads):
                head = slice(g * LANES + h * HEAD_SIZE, g * LANES + (h + 1) * HEAD_SIZE)
                mixed = jnp.dot(
                    values_ref[t, head],
                    weights_refs[held][g, :, h * seqs : (h + 1) * seqs],
                    preferred_element_type=F32,
                )
                gated_ref[t, head] = (mixed * gate_ref[t, head]).astype(BF16)

    score(0, 0)
    for t in range(tokens):
        if t > 0:
            mix(t - 1, (t - 1) % 2)
        weigh(t % 2)
        if t + 1 < tokens:
            score(t + 1, (t + 1) % 2)
    mix(tokens - 1, (tokens - 1) % 2)

    for t in range(tokens):
        delta = lax.dot_general(gated_ref[t], wo_ref[...], TN, preferred_element_type=F32)
        changed = (rows_of(xf_ref, t) + delta).astype(BF16).astype(F32)
        put_rows(hcf_ref, pl.ds(t, seqs, stride=tokens), changed)
        normed2 = standardize(changed, gains_ref[1:2, :]).astype(BF16)
        factors = lax.dot_general(wlr_ref[...], normed2, NT, preferred_element_type=F32)
        factors = factors * flag_ref[t]
        left_ref[t] = factors[:breadth].astype(BF16)
        rf_ref[pl.ds(t, breadth, stride=tokens), :] = factors[breadth:]

    hc_ref[...] = take_rows(hcf_ref, slice(None)).astype(BF16)
    right_ref[...] = rf_ref[...].astype(BF16)


def attention(x_rows, bias, flag_rows, gains, wqvg, wk, intercept, wo, wlr, tokens):
    rows, channels = x_rows.shape
    seqs = rows // tokens
    breadth = wlr.shape[0] // 2
    groups, group_heads = channels // LANES, LANES // HEAD_SIZE
    slab = pltpu.VMEM((channels // LANES, rows, LANES), F32)
    vmem = pl.BlockSpec(memory_space=pltpu.VMEM)
    return pl.pallas_call(
        functools.partial(attention_kernel, tokens),
        out_shape=(
            jax.ShapeDtypeStruct((rows, channels), BF16),
            jax.ShapeDtypeStruct((tokens, breadth, seqs), BF16),
            jax.ShapeDtypeStruct((breadth * tokens, seqs), BF16),
        ),
        in_specs=[vmem] * 9,
        out_specs=(vmem, vmem, vmem),
        scratch_shapes=[
            slab,
            slab,
            slab,
            pltpu.VMEM((breadth * tokens, seqs), F32),
            pltpu.VMEM((tokens, channels, seqs), BF16),
            pltpu.VMEM((tokens, seqs, channels), BF16),
            pltpu.VMEM((tokens, channels, seqs), BF16),
            pltpu.VMEM((tokens, channels, seqs), F32),
            pltpu.VMEM((tokens, channels, seqs), BF16),
        ]
        + [
            pltpu.VMEM((groups, seqs, group_heads * seqs), F32),
            pltpu.VMEM((groups, seqs, group_heads * seqs), BF16),
        ]
        * 2,
        compiler_params=pltpu.CompilerParams(vmem_limit_bytes=24 * 2**20),
        cost_estimate=pl.CostEstimate(
            flops=2 * rows * channels * (6 * channels),
            bytes_accessed=4 * rows * channels,
            transcendentals=0,
        ),
        name="attention",
    )(x_rows, bias, flag_rows, gains, wqvg, wk, intercept, wo, wlr)


def slot_of(block, stages):
    slot = 0
    for stride, size in reversed(stages):
        slot = slot * size + (block // stride) % size
    return slot


def pair_kernel(
    stages, per_device, me_ref, left_ref, right_ref, weight_ref, share_ref, base_ref, out_ref, outer_ref
):
    tok_local, breadth, seqs = left_ref.shape
    width = out_ref.shape[1]
    here = pl.program_id(0)
    devices_here = width // per_device
    me = me_ref[0]
    left = left_ref[...].reshape(tok_local * breadth, seqs)
    slots = [
        slot_of(jnp.bitwise_xor(me, here * devices_here + b), stages) for b in range(devices_here)
    ]

    for e in range(breadth):
        right = jnp.concatenate(
            [right_ref[slot, e * per_device : (e + 1) * per_device, :] for slot in slots], axis=0
        )
        outer = lax.dot_general(left, right, NT, preferred_element_type=F32).astype(BF16)
        outer_ref[:, e * breadth : (e + 1) * breadth, :] = outer.reshape(tok_local, breadth, width)

    for i in range(tok_local):
        projected = jnp.dot(weight_ref[...], outer_ref[i], preferred_element_type=F32)
        projected = projected * share_ref[i : i + 1, :]
        out_ref[i] = (base_ref[i] + projected.T).astype(BF16)


def pair_update(me, left, right_all, weight_t, share, base, stages):
    tok_local, breadth, seqs = left.shape
    pair_width = weight_t.shape[0]
    per_device = right_all.shape[1] // breadth
    columns = base.shape[1]
    width = min(columns, LANES)
    return pl.pallas_call(
        functools.partial(pair_kernel, stages, per_device),
        grid_spec=pltpu.PrefetchScalarGridSpec(
            num_scalar_prefetch=1,
            grid=(columns // width,),
            in_specs=[
                pl.BlockSpec(left.shape, lambda j, me: (0, 0, 0)),
                pl.BlockSpec(right_all.shape, lambda j, me: (0, 0, 0)),
                pl.BlockSpec(weight_t.shape, lambda j, me: (0, 0)),
                pl.BlockSpec((tok_local, width), lambda j, me: (0, j)),
                pl.BlockSpec((tok_local, width, pair_width), lambda j, me: (0, j, 0)),
            ],
            out_specs=pl.BlockSpec((tok_local, width, pair_width), lambda j, me: (0, j, 0)),
            scratch_shapes=[pltpu.VMEM((tok_local, breadth * breadth, width), BF16)],
        ),
        out_shape=jax.ShapeDtypeStruct(base.shape, BF16),
        compiler_params=pltpu.CompilerParams(vmem_limit_bytes=24 * 2**20),
        cost_estimate=pl.CostEstimate(
            flops=2 * tok_local * columns * breadth * breadth * (seqs + pair_width),
            bytes_accessed=8 * tok_local * columns * pair_width,
            transcendentals=0,
        ),
        name="pair_update",
    )(me, left, right_all, weight_t, share, base)


def gather_stages(size):
    chips = size // 2
    high = 2 ** math.ceil(math.log2(chips) / 2)
    low = chips // high
    return [(2 * low, high), (2, low), (1, 2)]


def gather_blocks(block, size, stages):
    held = block[None]
    for stride, members in stages:
        parts = [held]
        for k in range(1, members):
            pairs = [(d, d ^ (k * stride)) for d in range(size)]
            parts.append(lax.ppermute(held, "wide", pairs))
        held = jnp.concatenate(parts, axis=0)
    return held


def on_device(
    size,
    homolog_stack_state,
    present_flags,
    chain_ordinal_labels,
    pairwise_repr,
    heeding_normalizer_gains,
    retrieval_weights_qkv,
    logistic_weights,
    logistic_intercept,
    emitted_weights,
    dyadic_normalizer_gains,
    former_operand_weights,
    latter_operand_weights,
    flattened_outer_projection,
    clipped_separation_embedding,
):
    me = lax.axis_index("wide")
    seq_local, columns, channels = homolog_stack_state.shape
    tok_local = pairwise_repr.shape[0]
    seqs = seq_local * size
    breadth = former_operand_weights.shape[1]
    pair_width = flattened_outer_projection.shape[1]
    stages = gather_stages(size)

    sent = homolog_stack_state.reshape(seq_local, size, tok_local, channels).transpose(1, 0, 2, 3)
    x_rows = lax.all_to_all(sent, "wide", 0, 0, tiled=True).reshape(seqs * tok_local, channels)

    flags = present_flags.astype(F32)
    mine = lax.dynamic_slice_in_dim(flags, me * tok_local, tok_local, 1)
    flag_rows = mine.T[:, None, :]
    masks = (1000000000.0 * math.sqrt(HEAD_SIZE)) * (mine - 1.0)
    bias = jnp.pad(masks, ((0, 0), (0, LANES - tok_local))).astype(BF16)
    gains = jnp.stack([heeding_normalizer_gains, dyadic_normalizer_gains])
    weights_t = retrieval_weights_qkv.T
    wqvg = jnp.concatenate(
        [weights_t[:channels], weights_t[2 * channels :], logistic_weights.T], axis=0
    )
    wk = retrieval_weights_qkv[:, channels : 2 * channels]
    wlr = jnp.concatenate([former_operand_weights.T, latter_operand_weights.T], axis=0)
    projection_t = (
        flattened_outer_projection.reshape(breadth, breadth, pair_width)
        .transpose(2, 1, 0)
        .reshape(pair_width, breadth * breadth)
    )
    counts = jnp.dot(mine.T, flags, precision=lax.Precision.HIGHEST)
    share = 1.0 / counts
    labels_mine = lax.dynamic_slice_in_dim(chain_ordinal_labels, me * tok_local, tok_local, 0)
    offsets = (
        jnp.clip(labels_mine[:, None] - chain_ordinal_labels[None, :], -RELPOS_CLIP, RELPOS_CLIP)
        + RELPOS_CLIP
    )
    span = clipped_separation_embedding.shape[0]
    one_hot = (offsets[:, :, None] == jnp.arange(span, dtype=jnp.int32)[None, None, :]).astype(BF16)
    relpos = jnp.dot(
        one_hot.reshape(tok_local * columns, span),
        clipped_separation_embedding,
        preferred_element_type=F32,
    ).reshape(tok_local, columns, pair_width)
    base = pairwise_repr.astype(F32) + relpos

    x_rows, base, share, projection_t = lax.optimization_barrier(
        (x_rows, base, share, projection_t)
    )

    changed_rows, left, right = attention(
        x_rows,
        bias,
        flag_rows,
        gains,
        wqvg,
        wk,
        logistic_intercept[:, None],
        emitted_weights,
        wlr,
        tok_local,
    )

    right_all = gather_blocks(right, size, stages)
    back = lax.all_to_all(
        changed_rows.reshape(size, seq_local, tok_local, channels), "wide", 0, 0, tiled=True
    )
    homolog_changed = back.transpose(1, 0, 2, 3).reshape(seq_local, columns, channels)
    couple_state_changed = pair_update(
        me.reshape(1), left, right_all, projection_t, share, base, stages
    )
    return (homolog_changed, couple_state_changed)


def solution(mesh):
    in_specs = (
        P(("grp", "wide"), None, None),
        P("grp", None),
        P("grp"),
        P(("grp", "wide"), None, None),
    ) + (P(),) * 10
    out_specs = (P(("grp", "wide"), None, None), P(("grp", "wide"), None, None))
    return jax.shard_map(
        functools.partial(on_device, mesh.shape["wide"]),
        mesh=mesh,
        in_specs=in_specs,
        out_specs=out_specs,
        check_vma=False,
    )
```

```python
import functools
import math

import jax
import jax.numpy as jnp
from jax import lax
from jax.experimental import pallas as pl
from jax.experimental.pallas import tpu as pltpu
from jax.sharding import PartitionSpec as P


RELPOS_CLIP = 32
HEAD_SIZE = 32
EPSILON = 1e-05
LANES = 128
F32 = jnp.float32
BF16 = jnp.bfloat16


NT = (((1,), (1,)), ((), ()))
TN = (((0,), (0,)), ((), ()))


def standardize(values, gain_row):
    mean = jnp.mean(values, axis=-1, keepdims=True)
    centered = values - mean
    variance = jnp.mean(centered * centered, axis=-1, keepdims=True)
    return centered * lax.rsqrt(variance + EPSILON) * gain_row


def put_rows(ref, rows, values):
    for part in range(ref.shape[0]):
        ref[part, rows, :] = values[:, part * LANES : (part + 1) * LANES]


def take_rows(ref, rows):
    return jnp.concatenate([ref[part, rows, :] for part in range(ref.shape[0])], axis=1)


def attention_kernel(
    tokens,
    x_ref,
    bias_ref,
    flag_ref,
    gains_ref,
    wqvg_ref,
    wk_ref,
    intercept_ref,
    wo_ref,
    wlr_ref,
    hc_ref,
    left_ref,
    right_ref,
    xf_ref,
    normed_ref,
    hcf_ref,
    rf_ref,
    queries_ref,
    keys_ref,
    values_ref,
    gate_ref,
    gated_ref,
    *group_refs,
):
    logits_refs, weights_refs = group_refs[::2], group_refs[1::2]
    rows, channels = x_ref.shape
    seqs = rows // tokens
    breadth = wlr_ref.shape[0] // 2
    group_heads = LANES // HEAD_SIZE
    scale = math.log2(math.e) / math.sqrt(HEAD_SIZE)

    values = x_ref[...].astype(F32)
    put_rows(xf_ref, slice(None), values)
    put_rows(normed_ref, slice(None), standardize(values, gains_ref[0:1, :]))

    def rows_of(ref, t):
        return take_rows(ref, pl.ds(t, seqs, stride=tokens))

    normed = jnp.concatenate([rows_of(normed_ref, t) for t in range(tokens)], axis=0).astype(BF16)
    qvg = lax.dot_general(wqvg_ref[...], normed, NT, preferred_element_type=F32)
    keys = jnp.dot(normed, wk_ref[...], preferred_element_type=F32).astype(BF16)
    gate = 0.5 * jnp.tanh(0.5 * (qvg[2 * channels :] + intercept_ref[...])) + 0.5
    for t in range(tokens):
        at = slice(t * seqs, (t + 1) * seqs)
        queries_ref[t] = qvg[:channels, at].astype(BF16)
        values_ref[t] = qvg[channels : 2 * channels, at].astype(BF16)
        gate_ref[t] = gate[:, at]
        keys_ref[t] = keys[at]

    groups = channels // LANES

    def score(t, held):
        token_row = lax.broadcasted_iota(jnp.int32, (LANES, seqs), 0) == t
        token_row = jnp.where(token_row, 1.0, 0.0).astype(BF16)
        for g in range(groups):
            keys_g = jnp.concatenate(
                [keys_ref[t, :, g * LANES : (g + 1) * LANES], bias_ref[...]], axis=1
            )
            columns = []
            for h in range(group_heads):
                first = g * LANES + h * HEAD_SIZE
                parts = [queries_ref[t, first : first + HEAD_SIZE], token_row]
                above, below = h * HEAD_SIZE, LANES - (h + 1) * HEAD_SIZE
                if below:
                    parts.insert(1, jnp.zeros((below, seqs), BF16))
                if above:
                    parts.insert(0, jnp.zeros((above, seqs), BF16))
                columns.append(jnp.concatenate(parts, axis=0))
            logits_refs[held][g] = jnp.dot(
                keys_g, jnp.concatenate(columns, axis=1), preferred_element_type=F32
            )

    def weigh(held):
        for g in range(groups):
            for h in range(group_heads):
                head = slice(h * seqs, (h + 1) * seqs)
                logits = logits_refs[held][g, :, head]
                highest = jnp.max(logits, axis=0, keepdims=True)
                powers = jnp.exp2((logits - highest) * scale)
                share = 1.0 / jnp.sum(powers, axis=0, keepdims=True)
                weights_refs[held][g, :, head] = (powers * share).astype(BF16)

    def mix(t, held):
        for g in range(groups):
            for h in range(group_heads):
                head = slice(g * LANES + h * HEAD_SIZE, g * LANES + (h + 1) * HEAD_SIZE)
                mixed = jnp.dot(
                    values_ref[t, head],
                    weights_refs[held][g, :, h * seqs : (h + 1) * seqs],
                    preferred_element_type=F32,
                )
                gated_ref[t, head] = (mixed * gate_ref[t, head]).astype(BF16)

    score(0, 0)
    for t in range(tokens):
        if t > 0:
            mix(t - 1, (t - 1) % 2)
        weigh(t % 2)
        if t + 1 < tokens:
            score(t + 1, (t + 1) % 2)
    mix(tokens - 1, (tokens - 1) % 2)

    for t in range(tokens):
        delta = lax.dot_general(gated_ref[t], wo_ref[...], TN, preferred_element_type=F32)
        changed = (rows_of(xf_ref, t) + delta).astype(BF16).astype(F32)
        put_rows(hcf_ref, pl.ds(t, seqs, stride=tokens), changed)
        normed2 = standardize(changed, gains_ref[1:2, :]).astype(BF16)
        factors = lax.dot_general(wlr_ref[...], normed2, NT, preferred_element_type=F32)
        factors = factors * flag_ref[t]
        left_ref[t] = factors[:breadth].astype(BF16)
        rf_ref[pl.ds(t, breadth, stride=tokens), :] = factors[breadth:]

    hc_ref[...] = take_rows(hcf_ref, slice(None)).astype(BF16)
    right_ref[...] = rf_ref[...].astype(BF16)


def attention(x_rows, bias, flag_rows, gains, wqvg, wk, intercept, wo, wlr, tokens):
    rows, channels = x_rows.shape
    seqs = rows // tokens
    breadth = wlr.shape[0] // 2
    groups, group_heads = channels // LANES, LANES // HEAD_SIZE
    slab = pltpu.VMEM((channels // LANES, rows, LANES), F32)
    vmem = pl.BlockSpec(memory_space=pltpu.VMEM)
    return pl.pallas_call(
        functools.partial(attention_kernel, tokens),
        out_shape=(
            jax.ShapeDtypeStruct((rows, channels), BF16),
            jax.ShapeDtypeStruct((tokens, breadth, seqs), BF16),
            jax.ShapeDtypeStruct((breadth * tokens, seqs), BF16),
        ),
        in_specs=[vmem] * 9,
        out_specs=(vmem, vmem, vmem),
        scratch_shapes=[
            slab,
            slab,
            slab,
            pltpu.VMEM((breadth * tokens, seqs), F32),
            pltpu.VMEM((tokens, channels, seqs), BF16),
            pltpu.VMEM((tokens, seqs, channels), BF16),
            pltpu.VMEM((tokens, channels, seqs), BF16),
            pltpu.VMEM((tokens, channels, seqs), F32),
            pltpu.VMEM((tokens, channels, seqs), BF16),
        ]
        + [
            pltpu.VMEM((groups, seqs, group_heads * seqs), F32),
            pltpu.VMEM((groups, seqs, group_heads * seqs), BF16),
        ]
        * 2,
        compiler_params=pltpu.CompilerParams(vmem_limit_bytes=24 * 2**20),
        cost_estimate=pl.CostEstimate(
            flops=2 * rows * channels * (6 * channels),
            bytes_accessed=4 * rows * channels,
            transcendentals=0,
        ),
        name="attention",
    )(x_rows, bias, flag_rows, gains, wqvg, wk, intercept, wo, wlr)


def pair_kernel(
    stages, per_device, me_ref, left_ref, weight_ref, share_ref, base_ref, *refs
):
    held_refs, (out_ref, right_ref, outer_ref) = refs[:-3], refs[-3:]
    tok_local, breadth, seqs = left_ref.shape
    width = out_ref.shape[1]
    first = pl.program_id(0) * (width // per_device)
    me = me_ref[0]
    (far, far_size), (near, near_size), (core, core_size) = stages

    @pl.when(pl.program_id(0) == 0)
    def _():
        for n in range(near_size):
            for c in range(core_size):
                for f in range(far_size):
                    device = jnp.bitwise_xor(me, f * far + n * near + c * core)
                    right_ref[device] = held_refs[n * core_size + c][f]

    left = left_ref[...].reshape(tok_local * breadth, seqs)
    for e in range(breadth):
        right = jnp.concatenate(
            [
                right_ref[first + d, e * per_device : (e + 1) * per_device, :]
                for d in range(width // per_device)
            ],
            axis=0,
        )
        outer = lax.dot_general(left, right, NT, preferred_element_type=F32).astype(BF16)
        outer_ref[:, e * breadth : (e + 1) * breadth, :] = outer.reshape(tok_local, breadth, width)

    for i in range(tok_local):
        projected = jnp.dot(weight_ref[...], outer_ref[i], preferred_element_type=F32)
        projected = projected * share_ref[i : i + 1, :]
        out_ref[i] = (base_ref[i] + projected.T).astype(BF16)


def pair_update(me, left, right_held, weight_t, share, base, stages):
    tok_local, breadth, seqs = left.shape
    pair_width = weight_t.shape[0]
    block = right_held[0].shape[1:]
    per_device = block[0] // breadth
    columns = base.shape[1]
    width = min(columns, LANES)
    return pl.pallas_call(
        functools.partial(pair_kernel, stages, per_device),
        grid_spec=pltpu.PrefetchScalarGridSpec(
            num_scalar_prefetch=1,
            grid=(columns // width,),
            in_specs=[
                pl.BlockSpec(left.shape, lambda j, me: (0, 0, 0)),
                pl.BlockSpec(weight_t.shape, lambda j, me: (0, 0)),
                pl.BlockSpec((tok_local, width), lambda j, me: (0, j)),
                pl.BlockSpec((tok_local, width, pair_width), lambda j, me: (0, j, 0)),
            ]
            + [pl.BlockSpec(held.shape, lambda j, me: (0, 0, 0)) for held in right_held],
            out_specs=pl.BlockSpec((tok_local, width, pair_width), lambda j, me: (0, j, 0)),
            scratch_shapes=[
                pltpu.VMEM((columns // per_device, *block), BF16),
                pltpu.VMEM((tok_local, breadth * breadth, width), BF16),
            ],
        ),
        out_shape=jax.ShapeDtypeStruct(base.shape, BF16),
        compiler_params=pltpu.CompilerParams(
            vmem_limit_bytes=16 * 2**20 + 5 * columns * breadth * seqs * 2
        ),
        cost_estimate=pl.CostEstimate(
            flops=2 * tok_local * columns * breadth * breadth * (seqs + pair_width),
            bytes_accessed=8 * tok_local * columns * pair_width,
            transcendentals=0,
        ),
        name="pair_update",
    )(me, left, weight_t, share, base, *right_held)


def gather_stages(size):
    chips = size // 2
    high = 2 ** math.ceil(math.log2(chips) / 2)
    low = chips // high
    return [(2 * low, high), (2, low), (1, 2)]


def exchange(held, size, distance):
    return lax.ppermute(held, "wide", [(d, d ^ distance) for d in range(size)])


def gather_blocks(block, size, stages):
    (far, far_size), (near, near_size), (core, core_size) = stages
    block = block[None]
    column = jnp.concatenate(
        [block] + [exchange(block, size, f * far) for f in range(1, far_size)], axis=0
    )
    held = []
    for n in range(near_size):
        here = exchange(column, size, n * near) if n else column
        held += [here] + [exchange(here, size, c * core) for c in range(1, core_size)]
    return held


def on_device(
    size,
    homolog_stack_state,
    present_flags,
    chain_ordinal_labels,
    pairwise_repr,
    heeding_normalizer_gains,
    retrieval_weights_qkv,
    logistic_weights,
    logistic_intercept,
    emitted_weights,
    dyadic_normalizer_gains,
    former_operand_weights,
    latter_operand_weights,
    flattened_outer_projection,
    clipped_separation_embedding,
):
    me = lax.axis_index("wide")
    seq_local, columns, channels = homolog_stack_state.shape
    tok_local = pairwise_repr.shape[0]
    seqs = seq_local * size
    breadth = former_operand_weights.shape[1]
    pair_width = flattened_outer_projection.shape[1]
    stages = gather_stages(size)

    sent = homolog_stack_state.reshape(seq_local, size, tok_local, channels).transpose(1, 0, 2, 3)
    x_rows = lax.all_to_all(sent, "wide", 0, 0, tiled=True).reshape(seqs * tok_local, channels)

    flags = present_flags.astype(F32)
    mine = lax.dynamic_slice_in_dim(flags, me * tok_local, tok_local, 1)
    flag_rows = mine.T[:, None, :]
    masks = (1000000000.0 * math.sqrt(HEAD_SIZE)) * (mine - 1.0)
    bias = jnp.pad(masks, ((0, 0), (0, LANES - tok_local))).astype(BF16)
    gains = jnp.stack([heeding_normalizer_gains, dyadic_normalizer_gains])
    weights_t = retrieval_weights_qkv.T
    wqvg = jnp.concatenate(
        [weights_t[:channels], weights_t[2 * channels :], logistic_weights.T], axis=0
    )
    wk = retrieval_weights_qkv[:, channels : 2 * channels]
    wlr = jnp.concatenate([former_operand_weights.T, latter_operand_weights.T], axis=0)
    projection_t = (
        flattened_outer_projection.reshape(breadth, breadth, pair_width)
        .transpose(2, 1, 0)
        .reshape(pair_width, breadth * breadth)
    )
    counts = jnp.dot(mine.T, flags, precision=lax.Precision.HIGHEST)
    share = 1.0 / counts
    labels_mine = lax.dynamic_slice_in_dim(chain_ordinal_labels, me * tok_local, tok_local, 0)
    offsets = (
        jnp.clip(labels_mine[:, None] - chain_ordinal_labels[None, :], -RELPOS_CLIP, RELPOS_CLIP)
        + RELPOS_CLIP
    )
    span = clipped_separation_embedding.shape[0]
    one_hot = (offsets[:, :, None] == jnp.arange(span, dtype=jnp.int32)[None, None, :]).astype(BF16)
    relpos = jnp.dot(
        one_hot.reshape(tok_local * columns, span),
        clipped_separation_embedding,
        preferred_element_type=F32,
    ).reshape(tok_local, columns, pair_width)
    base = pairwise_repr.astype(F32) + relpos

    x_rows, base, share, projection_t = lax.optimization_barrier(
        (x_rows, base, share, projection_t)
    )

    changed_rows, left, right = attention(
        x_rows,
        bias,
        flag_rows,
        gains,
        wqvg,
        wk,
        logistic_intercept[:, None],
        emitted_weights,
        wlr,
        tok_local,
    )

    right_held = gather_blocks(right, size, stages)
    back = lax.all_to_all(
        changed_rows.reshape(size, seq_local, tok_local, channels), "wide", 0, 0, tiled=True
    )
    homolog_changed = back.transpose(1, 0, 2, 3).reshape(seq_local, columns, channels)
    couple_state_changed = pair_update(
        me.reshape(1), left, right_held, projection_t, share, base, stages
    )
    return (homolog_changed, couple_state_changed)


def solution(mesh):
    in_specs = (
        P(("grp", "wide"), None, None),
        P("grp", None),
        P("grp"),
        P(("grp", "wide"), None, None),
    ) + (P(),) * 10
    out_specs = (P(("grp", "wide"), None, None), P(("grp", "wide"), None, None))
    return jax.shard_map(
        functools.partial(on_device, mesh.shape["wide"]),
        mesh=mesh,
        in_specs=in_specs,
        out_specs=out_specs,
        check_vma=False,
    )
```

```python
import functools
import math

import jax
import jax.numpy as jnp
from jax import lax
from jax.experimental import pallas as pl
from jax.experimental.pallas import tpu as pltpu
from jax.sharding import PartitionSpec as P


RELPOS_CLIP = 32
HEAD_SIZE = 32
EPSILON = 1e-05
LANES = 128
F32 = jnp.float32
BF16 = jnp.bfloat16


NT = (((1,), (1,)), ((), ()))
TN = (((0,), (0,)), ((), ()))


def standardize(values, gain_row):
    mean = jnp.mean(values, axis=-1, keepdims=True)
    centered = values - mean
    variance = jnp.mean(centered * centered, axis=-1, keepdims=True)
    return centered * lax.rsqrt(variance + EPSILON) * gain_row


def put_rows(ref, rows, values):
    for part in range(ref.shape[0]):
        ref[part, rows, :] = values[:, part * LANES : (part + 1) * LANES]


def take_rows(ref, rows):
    return jnp.concatenate([ref[part, rows, :] for part in range(ref.shape[0])], axis=1)


def attention_kernel(
    tokens,
    x_ref,
    bias_ref,
    flag_ref,
    gains_ref,
    wqvg_ref,
    wk_ref,
    intercept_ref,
    wo_ref,
    wlr_ref,
    hc_ref,
    left_ref,
    right_ref,
    xf_ref,
    normed_ref,
    hcf_ref,
    rf_ref,
    queries_ref,
    keys_ref,
    values_ref,
    gate_ref,
    gated_ref,
    *group_refs,
):
    logits_refs, weights_refs = group_refs[::2], group_refs[1::2]
    rows, channels = x_ref.shape
    seqs = rows // tokens
    breadth = wlr_ref.shape[0] // 2
    group_heads = LANES // HEAD_SIZE
    scale = math.log2(math.e) / math.sqrt(HEAD_SIZE)

    values = x_ref[...].astype(F32)
    put_rows(xf_ref, slice(None), values)
    put_rows(normed_ref, slice(None), standardize(values, gains_ref[0:1, :]))

    def rows_of(ref, t):
        return take_rows(ref, pl.ds(t, seqs, stride=tokens))

    normed = jnp.concatenate([rows_of(normed_ref, t) for t in range(tokens)], axis=0).astype(BF16)
    qvg = lax.dot_general(wqvg_ref[...], normed, NT, preferred_element_type=F32)
    keys = jnp.dot(normed, wk_ref[...], preferred_element_type=F32).astype(BF16)
    gate = 0.5 * jnp.tanh(0.5 * (qvg[2 * channels :] + intercept_ref[...])) + 0.5
    for t in range(tokens):
        at = slice(t * seqs, (t + 1) * seqs)
        queries_ref[t] = qvg[:channels, at].astype(BF16)
        values_ref[t] = qvg[channels : 2 * channels, at].astype(BF16)
        gate_ref[t] = gate[:, at]
        keys_ref[t] = keys[at]

    groups = channels // LANES

    def score(t, held):
        token_row = lax.broadcasted_iota(jnp.int32, (LANES, seqs), 0) == t
        token_row = jnp.where(token_row, 1.0, 0.0).astype(BF16)
        for g in range(groups):
            keys_g = jnp.concatenate(
                [keys_ref[t, :, g * LANES : (g + 1) * LANES], bias_ref[...]], axis=1
            )
            columns = []
            for h in range(group_heads):
                first = g * LANES + h * HEAD_SIZE
                parts = [queries_ref[t, first : first + HEAD_SIZE], token_row]
                above, below = h * HEAD_SIZE, LANES - (h + 1) * HEAD_SIZE
                if below:
                    parts.insert(1, jnp.zeros((below, seqs), BF16))
                if above:
                    parts.insert(0, jnp.zeros((above, seqs), BF16))
                columns.append(jnp.concatenate(parts, axis=0))
            logits_refs[held][g] = jnp.dot(
                keys_g, jnp.concatenate(columns, axis=1), preferred_element_type=F32
            )

    def weigh(held):
        for g in range(groups):
            for h in range(group_heads):
                head = slice(h * seqs, (h + 1) * seqs)
                logits = logits_refs[held][g, :, head]
                highest = jnp.max(logits, axis=0, keepdims=True)
                powers = jnp.exp2((logits - highest) * scale)
                share = 1.0 / jnp.sum(powers, axis=0, keepdims=True)
                weights_refs[held][g, :, head] = (powers * share).astype(BF16)

    def mix(t, held):
        for g in range(groups):
            for h in range(group_heads):
                head = slice(g * LANES + h * HEAD_SIZE, g * LANES + (h + 1) * HEAD_SIZE)
                mixed = jnp.dot(
                    values_ref[t, head],
                    weights_refs[held][g, :, h * seqs : (h + 1) * seqs],
                    preferred_element_type=F32,
                )
                gated_ref[t, head] = (mixed * gate_ref[t, head]).astype(BF16)

    score(0, 0)
    for t in range(tokens):
        if t > 0:
            mix(t - 1, (t - 1) % 2)
        weigh(t % 2)
        if t + 1 < tokens:
            score(t + 1, (t + 1) % 2)
    mix(tokens - 1, (tokens - 1) % 2)

    for t in range(tokens):
        delta = lax.dot_general(gated_ref[t], wo_ref[...], TN, preferred_element_type=F32)
        changed = (rows_of(xf_ref, t) + delta).astype(BF16).astype(F32)
        put_rows(hcf_ref, pl.ds(t, seqs, stride=tokens), changed)
        normed2 = standardize(changed, gains_ref[1:2, :]).astype(BF16)
        factors = lax.dot_general(wlr_ref[...], normed2, NT, preferred_element_type=F32)
        factors = factors * flag_ref[t]
        left_ref[t] = factors[:breadth].astype(BF16)
        rf_ref[pl.ds(t, breadth, stride=tokens), :] = factors[breadth:]

    hc_ref[...] = take_rows(hcf_ref, slice(None)).astype(BF16)
    right_ref[...] = rf_ref[...].astype(BF16)


def attention(x_rows, bias, flag_rows, gains, wqvg, wk, intercept, wo, wlr, tokens):
    rows, channels = x_rows.shape
    seqs = rows // tokens
    breadth = wlr.shape[0] // 2
    groups, group_heads = channels // LANES, LANES // HEAD_SIZE
    slab = pltpu.VMEM((channels // LANES, rows, LANES), F32)
    vmem = pl.BlockSpec(memory_space=pltpu.VMEM)
    return pl.pallas_call(
        functools.partial(attention_kernel, tokens),
        out_shape=(
            jax.ShapeDtypeStruct((rows, channels), BF16),
            jax.ShapeDtypeStruct((tokens, breadth, seqs), BF16),
            jax.ShapeDtypeStruct((breadth * tokens, seqs), BF16),
        ),
        in_specs=[vmem] * 9,
        out_specs=(vmem, vmem, vmem),
        scratch_shapes=[
            slab,
            slab,
            slab,
            pltpu.VMEM((breadth * tokens, seqs), F32),
            pltpu.VMEM((tokens, channels, seqs), BF16),
            pltpu.VMEM((tokens, seqs, channels), BF16),
            pltpu.VMEM((tokens, channels, seqs), BF16),
            pltpu.VMEM((tokens, channels, seqs), F32),
            pltpu.VMEM((tokens, channels, seqs), BF16),
        ]
        + [
            pltpu.VMEM((groups, seqs, group_heads * seqs), F32),
            pltpu.VMEM((groups, seqs, group_heads * seqs), BF16),
        ]
        * 2,
        compiler_params=pltpu.CompilerParams(vmem_limit_bytes=24 * 2**20),
        cost_estimate=pl.CostEstimate(
            flops=2 * rows * channels * (6 * channels),
            bytes_accessed=4 * rows * channels,
            transcendentals=0,
        ),
        name="attention",
    )(x_rows, bias, flag_rows, gains, wqvg, wk, intercept, wo, wlr)


def pair_kernel(
    stages, distance, me_ref, left_ref, weight_ref, share_ref, base_ref, *refs
):
    (far, far_size), (near, near_size), (core, core_size) = stages
    held_refs, refs = refs[:core_size], refs[core_size:]
    last = distance == near_size - 1
    if last:
        done_refs, refs = refs[:-8], refs[-8:]
        back_ref, out_ref, changed_ref, right_ref, outer_ref, whole_ref, pair_ref, sems = refs
        devices, sequences = back_ref.shape[:2]
        for d in range(devices):
            for n in range(sequences):
                whole_ref[n, d] = back_ref[d, n]
        copies = [pltpu.make_async_copy(whole_ref, changed_ref, sems.at[left_ref.shape[0]])]
        copies[0].start()
    else:
        done_refs, (out_ref, right_ref, outer_ref) = (), refs
    tok_local, breadth, seqs = left_ref.shape
    per_device = held_refs[0].shape[1] // breadth
    chunk = core_size * per_device
    width = far_size * chunk
    pack = max(1, LANES // width)
    me = me_ref[0]
    my_far = jnp.bitwise_and(me // far, far_size - 1)
    my_near = jnp.bitwise_and(me // near, near_size - 1)
    my_core = jnp.bitwise_and(me // core, core_size - 1)

    def rows_at(f, n):
        chip = f * near_size + jnp.bitwise_xor(my_near, n)
        return pl.ds(pl.multiple_of(chip * chunk, chunk), chunk)

    for c in range(core_size):
        for f in range(far_size):
            device = jnp.bitwise_xor(my_far, f) * core_size + jnp.bitwise_xor(my_core, c)
            right_ref[device] = held_refs[c][f]

    left = left_ref[...].reshape(tok_local // pack, pack, breadth, seqs)
    left = jnp.concatenate(
        [left[:, k].reshape(tok_local // pack * breadth, seqs) for k in range(pack)], axis=1
    )
    nothing = jnp.zeros((width, seqs), BF16)
    step = 2 if breadth % 2 == 0 else 1
    for e in range(0, breadth, step):
        rows = []
        for k in range(e, e + step):
            right = jnp.concatenate(
                [
                    right_ref[d, k * per_device : (k + 1) * per_device, :]
                    for d in range(far_size * core_size)
                ],
                axis=0,
            )
            rows += [
                jnp.concatenate([right if j == k2 else nothing for j in range(pack)], axis=1)
                for k2 in range(pack)
            ]
        outer = lax.dot_general(
            left, jnp.concatenate(rows, axis=0), NT, preferred_element_type=F32
        ).astype(BF16)
        lanes = pack * width
        for k in range(step):
            outer_ref[:, (e + k) * breadth : (e + k + 1) * breadth, :] = outer[
                :, k * lanes : (k + 1) * lanes
            ].reshape(tok_local // pack, breadth, lanes)

    share = share_ref[jnp.bitwise_xor(my_near, distance)]
    for q in range(tok_local // pack):
        projected = jnp.dot(weight_ref[...], outer_ref[q], preferred_element_type=F32)
        projected = (projected * share[q : q + 1]).T
        for k in range(pack):
            i = q * pack + k
            for f in range(far_size):
                here = rows_at(f, distance)
                mine = projected[k * width + f * chunk : k * width + (f + 1) * chunk]
                value = (base_ref[i, here, :] + mine).astype(BF16)
                if last:
                    pair_ref[i, here, :] = value
                else:
                    out_ref[i, f * chunk : (f + 1) * chunk, :] = value
            for n, done_ref in enumerate(done_refs):
                for f in range(far_size):
                    pair_ref[i, rows_at(f, n), :] = done_ref[i, f * chunk : (f + 1) * chunk, :]
            if last:
                copies.append(pltpu.make_async_copy(pair_ref.at[i], out_ref.at[i], sems.at[i]))
                copies[-1].start()
    if last:
        for copy in copies:
            copy.wait()


def pair_part(distance, me, left, weight_t, share, base, held, done, back, stages):
    tok_local, breadth, seqs = left.shape
    pair_width = weight_t.shape[0]
    far_size, block = held[0].shape[0], held[0].shape[1:]
    columns = base.shape[1]
    width = columns // stages[1][1]
    pack = max(1, LANES // width)
    size, seq_local, _, channels = back.shape
    last = distance == stages[1][1] - 1
    vmem = pl.BlockSpec(memory_space=pltpu.VMEM)
    scratch = [
        pltpu.VMEM((far_size * len(held), *block), BF16),
        pltpu.VMEM((tok_local // pack, breadth * breadth, pack * width), BF16),
    ]
    out_shape = jax.ShapeDtypeStruct((tok_local, width, pair_width), BF16)
    out_specs = vmem
    operands = [left, weight_t, share, base, *held]
    if last:
        operands += [*done, back]
        out_shape = (
            jax.ShapeDtypeStruct(base.shape, BF16),
            jax.ShapeDtypeStruct((seq_local, size, tok_local, channels), BF16),
        )
        out_specs = (pl.BlockSpec(memory_space=pl.ANY), pl.BlockSpec(memory_space=pl.ANY))
        scratch += [
            pltpu.VMEM((seq_local, size, tok_local, channels), BF16),
            pltpu.VMEM(base.shape, BF16),
            pltpu.SemaphoreType.DMA((tok_local + 1,)),
        ]
    return pl.pallas_call(
        functools.partial(pair_kernel, stages, distance),
        in_specs=[pl.BlockSpec(memory_space=pltpu.SMEM)] + [vmem] * len(operands),
        out_specs=out_specs,
        scratch_shapes=scratch,
        out_shape=out_shape,
        compiler_params=pltpu.CompilerParams(
            vmem_limit_bytes=16 * 2**20 + 12 * tok_local * columns * pair_width
        ),
        cost_estimate=pl.CostEstimate(
            flops=2 * tok_local * width * breadth * breadth * (seqs + pair_width),
            bytes_accessed=8 * tok_local * width * pair_width,
            transcendentals=0,
        ),
        name="pair_part",
    )(me, *operands)


def gather_stages(size):
    chips = size // 2
    high = 2 ** math.ceil(math.log2(chips) / 2)
    low = chips // high
    return [(2 * low, high), (2, low), (1, 2)]


def exchange(held, size, distance):
    return lax.ppermute(held, "wide", [(d, d ^ distance) for d in range(size)])


def gather_blocks(block, size, stages):
    (far, far_size), (near, near_size), (core, core_size) = stages
    block = block[None]
    column = jnp.concatenate(
        [block] + [exchange(block, size, f * far) for f in range(1, far_size)], axis=0
    )
    held = []
    for n in range(near_size):
        here = exchange(column, size, n * near) if n else column
        held.append([here] + [exchange(here, size, c * core) for c in range(1, core_size)])
    return held


def on_device(
    size,
    homolog_stack_state,
    present_flags,
    chain_ordinal_labels,
    pairwise_repr,
    heeding_normalizer_gains,
    retrieval_weights_qkv,
    logistic_weights,
    logistic_intercept,
    emitted_weights,
    dyadic_normalizer_gains,
    former_operand_weights,
    latter_operand_weights,
    flattened_outer_projection,
    clipped_separation_embedding,
):
    me = lax.axis_index("wide")
    seq_local, columns, channels = homolog_stack_state.shape
    tok_local = pairwise_repr.shape[0]
    seqs = seq_local * size
    breadth = former_operand_weights.shape[1]
    pair_width = flattened_outer_projection.shape[1]
    stages = gather_stages(size)

    sent = homolog_stack_state.reshape(seq_local, size, tok_local, channels).transpose(1, 0, 2, 3)
    x_rows = lax.all_to_all(sent, "wide", 0, 0, tiled=True).reshape(seqs * tok_local, channels)

    flags = present_flags.astype(F32)
    mine = lax.dynamic_slice_in_dim(flags, me * tok_local, tok_local, 1)
    flag_rows = mine.T[:, None, :]
    masks = (1000000000.0 * math.sqrt(HEAD_SIZE)) * (mine - 1.0)
    bias = jnp.pad(masks, ((0, 0), (0, LANES - tok_local))).astype(BF16)
    gains = jnp.stack([heeding_normalizer_gains, dyadic_normalizer_gains])
    weights_t = retrieval_weights_qkv.T
    wqvg = jnp.concatenate(
        [weights_t[:channels], weights_t[2 * channels :], logistic_weights.T], axis=0
    )
    wk = retrieval_weights_qkv[:, channels : 2 * channels]
    wlr = jnp.concatenate([former_operand_weights.T, latter_operand_weights.T], axis=0)
    projection_t = (
        flattened_outer_projection.reshape(breadth, breadth, pair_width)
        .transpose(2, 1, 0)
        .reshape(pair_width, breadth * breadth)
    )
    counts = jnp.dot(mine.T, flags, precision=lax.Precision.HIGHEST)
    far_size, near_size = stages[0][1], stages[1][1]
    pack = max(1, LANES * near_size // columns)
    share = (1.0 / counts).reshape(tok_local, far_size, near_size, -1).transpose(2, 0, 1, 3)
    share = share.reshape(near_size, tok_local // pack, pack * columns // near_size)
    labels_mine = lax.dynamic_slice_in_dim(chain_ordinal_labels, me * tok_local, tok_local, 0)
    offsets = (
        jnp.clip(labels_mine[:, None] - chain_ordinal_labels[None, :], -RELPOS_CLIP, RELPOS_CLIP)
        + RELPOS_CLIP
    )
    span = clipped_separation_embedding.shape[0]
    one_hot = (offsets[:, :, None] == jnp.arange(span, dtype=jnp.int32)[None, None, :]).astype(BF16)
    relpos = jnp.dot(
        one_hot.reshape(tok_local * columns, span),
        clipped_separation_embedding,
        preferred_element_type=F32,
    ).reshape(tok_local, columns, pair_width)
    base = pairwise_repr.astype(F32) + relpos

    x_rows, base, share, projection_t = lax.optimization_barrier(
        (x_rows, base, share, projection_t)
    )

    changed_rows, left, right = attention(
        x_rows,
        bias,
        flag_rows,
        gains,
        wqvg,
        wk,
        logistic_intercept[:, None],
        emitted_weights,
        wlr,
        tok_local,
    )

    right_held = gather_blocks(right, size, stages)
    back = lax.all_to_all(
        changed_rows.reshape(size, seq_local, tok_local, channels), "wide", 0, 0, tiled=True
    )
    done = []
    for distance, held in enumerate(right_held):
        part = pair_part(
            distance,
            me.reshape(1),
            left,
            projection_t,
            share,
            base,
            held,
            done[:],
            back,
            stages,
        )
        done.append(part)
    couple_state_changed, homolog_changed = done[-1]
    return (homolog_changed.reshape(seq_local, columns, channels), couple_state_changed)


def solution(mesh):
    in_specs = (
        P(("grp", "wide"), None, None),
        P("grp", None),
        P("grp"),
        P(("grp", "wide"), None, None),
    ) + (P(),) * 10
    out_specs = (P(("grp", "wide"), None, None), P(("grp", "wide"), None, None))
    return jax.shard_map(
        functools.partial(on_device, mesh.shape["wide"]),
        mesh=mesh,
        in_specs=in_specs,
        out_specs=out_specs,
        check_vma=False,
    )
```

```python
import functools
import math

import jax
import jax.numpy as jnp
from jax import lax
from jax.experimental import pallas as pl
from jax.experimental.pallas import tpu as pltpu
from jax.sharding import PartitionSpec as P


RELPOS_CLIP = 32
HEAD_SIZE = 32
EPSILON = 1e-05
LANES = 128
F32 = jnp.float32
BF16 = jnp.bfloat16


NT = (((1,), (1,)), ((), ()))
TN = (((0,), (0,)), ((), ()))


def standardize(values, gain_row):
    mean = jnp.mean(values, axis=-1, keepdims=True)
    centered = values - mean
    variance = jnp.mean(centered * centered, axis=-1, keepdims=True)
    return centered * lax.rsqrt(variance + EPSILON) * gain_row


def put_rows(ref, rows, values):
    for part in range(ref.shape[0]):
        ref[part, rows, :] = values[:, part * LANES : (part + 1) * LANES]


def take_rows(ref, rows):
    return jnp.concatenate([ref[part, rows, :] for part in range(ref.shape[0])], axis=1)


def attention_kernel(
    tokens,
    x_ref,
    bias_ref,
    flag_ref,
    gains_ref,
    wqvg_ref,
    wk_ref,
    intercept_ref,
    wo_ref,
    wlr_ref,
    hc_ref,
    left_ref,
    right_ref,
    xf_ref,
    normed_ref,
    hcf_ref,
    rf_ref,
    queries_ref,
    keys_ref,
    values_ref,
    gate_ref,
    gated_ref,
    *group_refs,
):
    logits_refs, weights_refs = group_refs[::2], group_refs[1::2]
    rows, channels = x_ref.shape
    seqs = rows // tokens
    breadth = wlr_ref.shape[0] // 2
    group_heads = LANES // HEAD_SIZE
    scale = math.log2(math.e) / math.sqrt(HEAD_SIZE)

    values = x_ref[...].astype(F32)
    put_rows(xf_ref, slice(None), values)
    put_rows(normed_ref, slice(None), standardize(values, gains_ref[0:1, :]))

    def rows_of(ref, t):
        return take_rows(ref, pl.ds(t, seqs, stride=tokens))

    def project(first, count):
        near = range(first, first + count)
        normed = jnp.concatenate([rows_of(normed_ref, t) for t in near], axis=0).astype(BF16)
        qvg = lax.dot_general(wqvg_ref[...], normed, NT, preferred_element_type=F32)
        keys = jnp.dot(normed, wk_ref[...], preferred_element_type=F32).astype(BF16)
        gate = 0.5 * jnp.tanh(0.5 * (qvg[2 * channels :] + intercept_ref[...])) + 0.5
        for k, t in enumerate(near):
            at = slice(k * seqs, (k + 1) * seqs)
            queries_ref[t] = qvg[:channels, at].astype(BF16)
            values_ref[t] = qvg[channels : 2 * channels, at].astype(BF16)
            gate_ref[t] = gate[:, at]
            keys_ref[t] = keys[at]

    groups = channels // LANES

    def score(t, held):
        token_row = lax.broadcasted_iota(jnp.int32, (LANES, seqs), 0) == t
        token_row = jnp.where(token_row, 1.0, 0.0).astype(BF16)
        for g in range(groups):
            keys_g = jnp.concatenate(
                [keys_ref[t, :, g * LANES : (g + 1) * LANES], bias_ref[...]], axis=1
            )
            columns = []
            for h in range(group_heads):
                first = g * LANES + h * HEAD_SIZE
                parts = [queries_ref[t, first : first + HEAD_SIZE], token_row]
                above, below = h * HEAD_SIZE, LANES - (h + 1) * HEAD_SIZE
                if below:
                    parts.insert(1, jnp.zeros((below, seqs), BF16))
                if above:
                    parts.insert(0, jnp.zeros((above, seqs), BF16))
                columns.append(jnp.concatenate(parts, axis=0))
            logits_refs[held][g] = jnp.dot(
                keys_g, jnp.concatenate(columns, axis=1), preferred_element_type=F32
            )

    def weigh(held):
        for g in range(groups):
            for h in range(group_heads):
                head = slice(h * seqs, (h + 1) * seqs)
                logits = logits_refs[held][g, :, head]
                highest = jnp.max(logits, axis=0, keepdims=True)
                powers = jnp.exp2((logits - highest) * scale)
                share = 1.0 / jnp.sum(powers, axis=0, keepdims=True)
                weights_refs[held][g, :, head] = (powers * share).astype(BF16)

    def mix(t, held):
        for g in range(groups):
            for h in range(group_heads):
                head = slice(g * LANES + h * HEAD_SIZE, g * LANES + (h + 1) * HEAD_SIZE)
                mixed = jnp.dot(
                    values_ref[t, head],
                    weights_refs[held][g, :, h * seqs : (h + 1) * seqs],
                    preferred_element_type=F32,
                )
                gated_ref[t, head] = (mixed * gate_ref[t, head]).astype(BF16)

    project(0, 2)
    score(0, 0)
    for t in range(tokens):
        if t % 2 == 0 and t + 2 < tokens:
            project(t + 2, 2)
        if t > 0:
            mix(t - 1, (t - 1) % 2)
        weigh(t % 2)
        if t + 1 < tokens:
            score(t + 1, (t + 1) % 2)
    mix(tokens - 1, (tokens - 1) % 2)

    for t in range(tokens):
        delta = lax.dot_general(gated_ref[t], wo_ref[...], TN, preferred_element_type=F32)
        changed = (rows_of(xf_ref, t) + delta).astype(BF16).astype(F32)
        put_rows(hcf_ref, pl.ds(t, seqs, stride=tokens), changed)
        normed2 = standardize(changed, gains_ref[1:2, :]).astype(BF16)
        factors = lax.dot_general(wlr_ref[...], normed2, NT, preferred_element_type=F32)
        factors = factors * flag_ref[t]
        left_ref[t] = factors[:breadth].astype(BF16)
        rf_ref[pl.ds(t, breadth, stride=tokens), :] = factors[breadth:]

    hc_ref[...] = take_rows(hcf_ref, slice(None)).astype(BF16)
    right_ref[...] = rf_ref[...].astype(BF16)


def attention(x_rows, bias, flag_rows, gains, wqvg, wk, intercept, wo, wlr, tokens):
    rows, channels = x_rows.shape
    seqs = rows // tokens
    breadth = wlr.shape[0] // 2
    groups, group_heads = channels // LANES, LANES // HEAD_SIZE
    slab = pltpu.VMEM((channels // LANES, rows, LANES), F32)
    vmem = pl.BlockSpec(memory_space=pltpu.VMEM)
    return pl.pallas_call(
        functools.partial(attention_kernel, tokens),
        out_shape=(
            jax.ShapeDtypeStruct((rows, channels), BF16),
            jax.ShapeDtypeStruct((tokens, breadth, seqs), BF16),
            jax.ShapeDtypeStruct((breadth * tokens, seqs), BF16),
        ),
        in_specs=[vmem] * 9,
        out_specs=(vmem, vmem, vmem),
        scratch_shapes=[
            slab,
            slab,
            slab,
            pltpu.VMEM((breadth * tokens, seqs), F32),
            pltpu.VMEM((tokens, channels, seqs), BF16),
            pltpu.VMEM((tokens, seqs, channels), BF16),
            pltpu.VMEM((tokens, channels, seqs), BF16),
            pltpu.VMEM((tokens, channels, seqs), F32),
            pltpu.VMEM((tokens, channels, seqs), BF16),
        ]
        + [
            pltpu.VMEM((groups, seqs, group_heads * seqs), F32),
            pltpu.VMEM((groups, seqs, group_heads * seqs), BF16),
        ]
        * 2,
        compiler_params=pltpu.CompilerParams(vmem_limit_bytes=24 * 2**20),
        cost_estimate=pl.CostEstimate(
            flops=2 * rows * channels * (6 * channels),
            bytes_accessed=4 * rows * channels,
            transcendentals=0,
        ),
        name="attention",
    )(x_rows, bias, flag_rows, gains, wqvg, wk, intercept, wo, wlr)


def digit(me, stage):
    stride, members = stage
    return jnp.bitwise_and(me // stride, members - 1)


def pair_kernel(
    stages, me_ref, left_ref, weight_ref, share_ref, base_ref, *refs
):
    far_stage, _, core_stage = stages
    far_size, core_size = far_stage[1], core_stage[1]
    held_refs, (out_ref, right_ref, outer_ref) = refs[:core_size], refs[core_size:]
    tok_local, breadth, seqs = left_ref.shape
    per_device = held_refs[0].shape[1] // breadth
    width = base_ref.shape[1]
    pack = max(1, LANES // width)
    me = me_ref[0]

    for c in range(core_size):
        for f in range(far_size):
            far, core = digit(me, far_stage), digit(me, core_stage)
            device = jnp.bitwise_xor(far, f) * core_size + jnp.bitwise_xor(core, c)
            right_ref[device] = held_refs[c][f]

    left = left_ref[...].reshape(tok_local // pack, pack, breadth, seqs)
    left = jnp.concatenate(
        [left[:, k].reshape(tok_local // pack * breadth, seqs) for k in range(pack)], axis=1
    )
    nothing = jnp.zeros((width, seqs), BF16)
    step = math.gcd(breadth, 2)
    for e in range(0, breadth, step):
        rows = []
        for k in range(e, e + step):
            right = jnp.concatenate(
                [
                    right_ref[d, k * per_device : (k + 1) * per_device, :]
                    for d in range(far_size * core_size)
                ],
                axis=0,
            )
            rows += [
                jnp.concatenate([right if j == k2 else nothing for j in range(pack)], axis=1)
                for k2 in range(pack)
            ]
        outer = lax.dot_general(
            left, jnp.concatenate(rows, axis=0), NT, preferred_element_type=F32
        ).astype(BF16)
        lanes = pack * width
        for k in range(step):
            outer_ref[:, (e + k) * breadth : (e + k + 1) * breadth, :] = outer[
                :, k * lanes : (k + 1) * lanes
            ].reshape(tok_local // pack, breadth, lanes)

    for q in range(tok_local // pack):
        projected = jnp.dot(weight_ref[...], outer_ref[q], preferred_element_type=F32)
        projected = (projected * share_ref[q : q + 1]).T
        for k in range(pack):
            i = q * pack + k
            mine = projected[k * width : (k + 1) * width]
            out_ref[i] = (base_ref[i] + mine).astype(BF16)


def pair_part(me, left, weight_t, share, base, held, stages):
    tok_local, breadth, seqs = left.shape
    pair_width = weight_t.shape[0]
    far_size, block = held[0].shape[0], held[0].shape[1:]
    width = base.shape[1]
    pack = max(1, LANES // width)
    vmem = pl.BlockSpec(memory_space=pltpu.VMEM)
    return pl.pallas_call(
        functools.partial(pair_kernel, stages),
        in_specs=[pl.BlockSpec(memory_space=pltpu.SMEM)] + [vmem] * (4 + len(held)),
        out_specs=vmem,
        scratch_shapes=[
            pltpu.VMEM((far_size * len(held), *block), BF16),
            pltpu.VMEM((tok_local // pack, breadth * breadth, pack * width), BF16),
        ],
        out_shape=jax.ShapeDtypeStruct(base.shape, BF16),
        compiler_params=pltpu.CompilerParams(vmem_limit_bytes=24 * 2**20),
        cost_estimate=pl.CostEstimate(
            flops=2 * tok_local * width * breadth * breadth * (seqs + pair_width),
            bytes_accessed=8 * tok_local * width * pair_width,
            transcendentals=0,
        ),
        name="pair_part",
    )(me, left, weight_t, share, base, *held)


def finish_kernel(stages, me_ref, back_ref, *refs):
    far_stage, near_stage, _ = stages
    near_size = near_stage[1]
    part_refs, refs = refs[:near_size], refs[near_size:]
    pair_out_ref, changed_out_ref, pair_ref, changed_ref, sems = refs
    devices, sequences = back_ref.shape[:2]
    for d in range(devices):
        for n in range(sequences):
            changed_ref[n, d] = back_ref[d, n]
    copies = [pltpu.make_async_copy(changed_ref, changed_out_ref, sems.at[0])]
    copies[0].start()
    chunk = part_refs[0].shape[1] // far_stage[1]
    near = digit(me_ref[0], near_stage)
    for n in range(near_size):
        for f in range(far_stage[1]):
            chip = f * near_size + jnp.bitwise_xor(near, n)
            here = pl.ds(pl.multiple_of(chip * chunk, chunk), chunk)
            pair_ref[:, here, :] = part_refs[n][:, f * chunk : (f + 1) * chunk, :]
    copies.append(pltpu.make_async_copy(pair_ref, pair_out_ref, sems.at[1]))
    copies[1].start()
    for copy in copies:
        copy.wait()


def finish(me, back, parts, stages):
    size, seq_local, tok_local, channels = back.shape
    rows, width, pair_width = parts[0].shape
    pair_shape = (rows, width * len(parts), pair_width)
    changed_shape = (seq_local, size, tok_local, channels)
    vmem, anywhere = pl.BlockSpec(memory_space=pltpu.VMEM), pl.BlockSpec(memory_space=pl.ANY)
    return pl.pallas_call(
        functools.partial(finish_kernel, stages),
        in_specs=[pl.BlockSpec(memory_space=pltpu.SMEM)] + [vmem] * (1 + len(parts)),
        out_specs=(anywhere, anywhere),
        scratch_shapes=[
            pltpu.VMEM(pair_shape, BF16),
            pltpu.VMEM(changed_shape, BF16),
            pltpu.SemaphoreType.DMA((2,)),
        ],
        out_shape=(
            jax.ShapeDtypeStruct(pair_shape, BF16),
            jax.ShapeDtypeStruct(changed_shape, BF16),
        ),
        compiler_params=pltpu.CompilerParams(vmem_limit_bytes=24 * 2**20),
        name="finish",
    )(me, back, *parts)


def gather_stages(size):
    chips = size // 2
    high = 2 ** math.ceil(math.log2(chips) / 2)
    low = chips // high
    return [(2 * low, high), (2, low), (1, 2)]


def exchange(held, size, distance):
    return lax.ppermute(held, "wide", [(d, d ^ distance) for d in range(size)])


def gather_column(block, size, stages):
    (far, far_size), _, (core, core_size) = stages
    block = block[None]
    column = jnp.concatenate(
        [block] + [exchange(block, size, f * far) for f in range(1, far_size)], axis=0
    )
    return [column] + [exchange(column, size, c * core) for c in range(1, core_size)]


def on_device(
    size,
    homolog_stack_state,
    present_flags,
    chain_ordinal_labels,
    pairwise_repr,
    heeding_normalizer_gains,
    retrieval_weights_qkv,
    logistic_weights,
    logistic_intercept,
    emitted_weights,
    dyadic_normalizer_gains,
    former_operand_weights,
    latter_operand_weights,
    flattened_outer_projection,
    clipped_separation_embedding,
):
    me = lax.axis_index("wide")
    seq_local, columns, channels = homolog_stack_state.shape
    tok_local = pairwise_repr.shape[0]
    seqs = seq_local * size
    breadth = former_operand_weights.shape[1]
    pair_width = flattened_outer_projection.shape[1]
    stages = gather_stages(size)

    sent = homolog_stack_state.reshape(seq_local, size, tok_local, channels).transpose(1, 0, 2, 3)
    x_rows = lax.all_to_all(sent, "wide", 0, 0, tiled=True)
    x_rows = x_rows.reshape(seqs * tok_local, channels)

    flags = present_flags.astype(F32)
    mine = lax.dynamic_slice_in_dim(flags, me * tok_local, tok_local, 1)
    flag_rows = mine.T[:, None, :]
    masks = (1000000000.0 * math.sqrt(HEAD_SIZE)) * (mine - 1.0)
    bias = jnp.pad(masks, ((0, 0), (0, LANES - tok_local))).astype(BF16)
    gains = jnp.stack([heeding_normalizer_gains, dyadic_normalizer_gains])
    weights_t = retrieval_weights_qkv.T
    wqvg = jnp.concatenate(
        [weights_t[:channels], weights_t[2 * channels :], logistic_weights.T], axis=0
    )
    wk = retrieval_weights_qkv[:, channels : 2 * channels]
    wlr = jnp.concatenate([former_operand_weights.T, latter_operand_weights.T], axis=0)
    projection_t = (
        flattened_outer_projection.reshape(breadth, breadth, pair_width)
        .transpose(2, 1, 0)
        .reshape(pair_width, breadth * breadth)
    )
    (_, far_size), (near, near_size), (_, core_size) = stages
    my_near = digit(me, stages[1])
    chunk = core_size * tok_local
    width = far_size * chunk
    pack = max(1, LANES // width)

    def near_columns(values, axis, near_digit):
        shape = values.shape
        split = values.reshape(shape[:axis] + (far_size, near_size, chunk) + shape[axis + 1 :])
        taken = lax.dynamic_index_in_dim(split, near_digit, axis + 1, keepdims=False)
        return taken.reshape(shape[:axis] + (width,) + shape[axis + 1 :])

    flags_here = near_columns(flags, 1, my_near)
    labels_here = near_columns(chain_ordinal_labels, 0, my_near)
    span = clipped_separation_embedding.shape[0]
    shares, bases = [], []
    for n in range(near_size):
        first = jnp.bitwise_xor(me, n * near) * tok_local
        rows_flags = lax.dynamic_slice_in_dim(flags, first, tok_local, 1)
        counts = jnp.dot(rows_flags.T, flags_here, precision=lax.Precision.HIGHEST)
        shares.append((1.0 / counts).reshape(tok_local // pack, pack * width))
        labels = lax.dynamic_slice_in_dim(chain_ordinal_labels, first, tok_local, 0)
        offsets = (
            jnp.clip(labels[:, None] - labels_here[None, :], -RELPOS_CLIP, RELPOS_CLIP)
            + RELPOS_CLIP
        )
        one_hot = (offsets[:, :, None] == jnp.arange(span, dtype=jnp.int32)[None, None, :]).astype(
            BF16
        )
        relpos = jnp.dot(
            one_hot.reshape(tok_local * width, span),
            clipped_separation_embedding,
            preferred_element_type=F32,
        ).reshape(tok_local, width, pair_width)
        entries = near_columns(pairwise_repr, 1, jnp.bitwise_xor(my_near, n))
        if n:
            entries = exchange(entries, size, n * near)
        bases.append(entries.astype(F32) + relpos)

    x_rows, bases, shares, projection_t = lax.optimization_barrier(
        (x_rows, bases, shares, projection_t)
    )

    changed_rows, left, right = attention(
        x_rows,
        bias,
        flag_rows,
        gains,
        wqvg,
        wk,
        logistic_intercept[:, None],
        emitted_weights,
        wlr,
        tok_local,
    )

    me = me.reshape(1)
    held = gather_column(right, size, stages)
    back = lax.all_to_all(
        changed_rows.reshape(size, seq_local, tok_local, channels), "wide", 0, 0, tiled=True
    )
    lefts = [left] + [exchange(left, size, n * near) for n in range(1, near_size)]
    parts = []
    for n in range(near_size):
        part = pair_part(me, lefts[n], projection_t, shares[n], bases[n], held, stages)
        parts.append(exchange(part, size, n * near) if n else part)
    couple_state_changed, homolog_changed = finish(me, back, parts, stages)
    return (homolog_changed.reshape(seq_local, columns, channels), couple_state_changed)


def solution(mesh):
    in_specs = (
        P(("grp", "wide"), None, None),
        P("grp", None),
        P("grp"),
        P(("grp", "wide"), None, None),
    ) + (P(),) * 10
    out_specs = (P(("grp", "wide"), None, None), P(("grp", "wide"), None, None))
    return jax.shard_map(
        functools.partial(on_device, mesh.shape["wide"]),
        mesh=mesh,
        in_specs=in_specs,
        out_specs=out_specs,
        check_vma=False,
    )
```

```python
import functools
import math

import jax
import jax.numpy as jnp
from jax import lax
from jax.experimental import pallas as pl
from jax.experimental.pallas import tpu as pltpu
from jax.sharding import PartitionSpec as P


RELPOS_CLIP = 32
HEAD_SIZE = 32
EPSILON = 1e-05
LANES = 128
F32 = jnp.float32
BF16 = jnp.bfloat16


NT = (((1,), (1,)), ((), ()))
TN = (((0,), (0,)), ((), ()))


def standardize(values, gain_row):
    mean = jnp.mean(values, axis=-1, keepdims=True)
    centered = values - mean
    variance = jnp.mean(centered * centered, axis=-1, keepdims=True)
    return centered * lax.rsqrt(variance + EPSILON) * gain_row


def put_rows(ref, rows, values):
    for part in range(ref.shape[0]):
        ref[part, rows, :] = values[:, part * LANES : (part + 1) * LANES]


def take_rows(ref, rows):
    return jnp.concatenate([ref[part, rows, :] for part in range(ref.shape[0])], axis=1)


def attention_kernel(
    tokens,
    x_ref,
    bias_ref,
    flag_ref,
    gains_ref,
    wqvg_ref,
    wk_ref,
    intercept_ref,
    wo_ref,
    wlr_ref,
    hc_ref,
    left_ref,
    right_ref,
    xf_ref,
    normed_ref,
    hcf_ref,
    rf_ref,
    queries_ref,
    keys_ref,
    values_ref,
    gate_ref,
    gated_ref,
    *group_refs,
):
    logits_refs, weights_refs = group_refs[::2], group_refs[1::2]
    rows, channels = x_ref.shape
    seqs = rows // tokens
    breadth = wlr_ref.shape[0] // 2
    group_heads = LANES // HEAD_SIZE
    scale = math.log2(math.e) / math.sqrt(HEAD_SIZE)

    values = x_ref[...].astype(F32)
    put_rows(xf_ref, slice(None), values)
    put_rows(normed_ref, slice(None), standardize(values, gains_ref[0:1, :]))

    def rows_of(ref, t):
        return take_rows(ref, pl.ds(t, seqs, stride=tokens))

    def project(first, count):
        near = range(first, first + count)
        normed = jnp.concatenate([rows_of(normed_ref, t) for t in near], axis=0).astype(BF16)
        qvg = lax.dot_general(wqvg_ref[...], normed, NT, preferred_element_type=F32)
        keys = jnp.dot(normed, wk_ref[...], preferred_element_type=F32).astype(BF16)
        gate = 0.5 * jnp.tanh(0.5 * (qvg[2 * channels :] + intercept_ref[...])) + 0.5
        for k, t in enumerate(near):
            at = slice(k * seqs, (k + 1) * seqs)
            queries_ref[t] = (qvg[:channels, at] * scale).astype(BF16)
            values_ref[t] = qvg[channels : 2 * channels, at].astype(BF16)
            gate_ref[t] = gate[:, at]
            keys_ref[t] = keys[at]

    groups = channels // LANES

    def score(t, held):
        token_row = lax.broadcasted_iota(jnp.int32, (LANES, seqs), 0) == t
        token_row = jnp.where(token_row, 1.0, 0.0).astype(BF16)
        for g in range(groups):
            keys_g = jnp.concatenate(
                [keys_ref[t, :, g * LANES : (g + 1) * LANES], bias_ref[...]], axis=1
            )
            columns = []
            for h in range(group_heads):
                first = g * LANES + h * HEAD_SIZE
                parts = [queries_ref[t, first : first + HEAD_SIZE], token_row]
                above, below = h * HEAD_SIZE, LANES - (h + 1) * HEAD_SIZE
                if below:
                    parts.insert(1, jnp.zeros((below, seqs), BF16))
                if above:
                    parts.insert(0, jnp.zeros((above, seqs), BF16))
                columns.append(jnp.concatenate(parts, axis=0))
            logits_refs[held][g] = jnp.dot(
                keys_g, jnp.concatenate(columns, axis=1), preferred_element_type=F32
            )

    def weigh(held):
        for g in range(groups):
            for h in range(group_heads):
                head = slice(h * seqs, (h + 1) * seqs)
                logits = logits_refs[held][g, :, head]
                highest = jnp.max(logits, axis=0, keepdims=True)
                powers = jnp.exp2(logits - highest)
                share = 1.0 / jnp.sum(powers, axis=0, keepdims=True)
                weights_refs[held][g, :, head] = (powers * share).astype(BF16)

    def mix(t, held):
        for g in range(groups):
            for h in range(group_heads):
                head = slice(g * LANES + h * HEAD_SIZE, g * LANES + (h + 1) * HEAD_SIZE)
                mixed = jnp.dot(
                    values_ref[t, head],
                    weights_refs[held][g, :, h * seqs : (h + 1) * seqs],
                    preferred_element_type=F32,
                )
                gated_ref[t, head] = (mixed * gate_ref[t, head]).astype(BF16)

    project(0, 2)
    score(0, 0)
    for t in range(tokens):
        if t % 2 == 0 and t + 2 < tokens:
            project(t + 2, 2)
        if t > 0:
            mix(t - 1, (t - 1) % 2)
        weigh(t % 2)
        if t + 1 < tokens:
            score(t + 1, (t + 1) % 2)
    mix(tokens - 1, (tokens - 1) % 2)

    for t in range(tokens):
        delta = lax.dot_general(gated_ref[t], wo_ref[...], TN, preferred_element_type=F32)
        changed = (rows_of(xf_ref, t) + delta).astype(BF16).astype(F32)
        put_rows(hcf_ref, pl.ds(t, seqs, stride=tokens), changed)
        normed2 = standardize(changed, gains_ref[1:2, :]).astype(BF16)
        factors = lax.dot_general(wlr_ref[...], normed2, NT, preferred_element_type=F32)
        factors = factors * flag_ref[t]
        left_ref[t] = factors[:breadth].astype(BF16)
        rf_ref[pl.ds(t, breadth, stride=tokens), :] = factors[breadth:]

    hc_ref[...] = take_rows(hcf_ref, slice(None)).astype(BF16)
    right_ref[...] = rf_ref[...].astype(BF16)


def attention(x_rows, bias, flag_rows, gains, wqvg, wk, intercept, wo, wlr, tokens):
    rows, channels = x_rows.shape
    seqs = rows // tokens
    breadth = wlr.shape[0] // 2
    groups, group_heads = channels // LANES, LANES // HEAD_SIZE
    slab = pltpu.VMEM((channels // LANES, rows, LANES), F32)
    vmem = pl.BlockSpec(memory_space=pltpu.VMEM)
    return pl.pallas_call(
        functools.partial(attention_kernel, tokens),
        out_shape=(
            jax.ShapeDtypeStruct((rows, channels), BF16),
            jax.ShapeDtypeStruct((tokens, breadth, seqs), BF16),
            jax.ShapeDtypeStruct((breadth * tokens, seqs), BF16),
        ),
        in_specs=[vmem] * 9,
        out_specs=(vmem, vmem, vmem),
        scratch_shapes=[
            slab,
            slab,
            slab,
            pltpu.VMEM((breadth * tokens, seqs), F32),
            pltpu.VMEM((tokens, channels, seqs), BF16),
            pltpu.VMEM((tokens, seqs, channels), BF16),
            pltpu.VMEM((tokens, channels, seqs), BF16),
            pltpu.VMEM((tokens, channels, seqs), F32),
            pltpu.VMEM((tokens, channels, seqs), BF16),
        ]
        + [
            pltpu.VMEM((groups, seqs, group_heads * seqs), F32),
            pltpu.VMEM((groups, seqs, group_heads * seqs), BF16),
        ]
        * 2,
        compiler_params=pltpu.CompilerParams(vmem_limit_bytes=24 * 2**20),
        cost_estimate=pl.CostEstimate(
            flops=2 * rows * channels * (6 * channels),
            bytes_accessed=4 * rows * channels,
            transcendentals=0,
        ),
        name="attention",
    )(x_rows, bias, flag_rows, gains, wqvg, wk, intercept, wo, wlr)


def digit(me, stage):
    stride, members = stage
    return jnp.bitwise_and(me // stride, members - 1)


def pair_kernel(
    stages, me_ref, left_ref, weight_ref, share_ref, base_ref, *refs
):
    far_stage, _, core_stage = stages
    far_size, core_size = far_stage[1], core_stage[1]
    held_refs, (out_ref, right_ref, outer_ref) = refs[:core_size], refs[core_size:]
    tok_local, breadth, seqs = left_ref.shape
    per_device = held_refs[0].shape[1] // breadth
    width = base_ref.shape[1]
    pack = max(1, LANES // width)
    me = me_ref[0]

    for c in range(core_size):
        for f in range(far_size):
            far, core = digit(me, far_stage), digit(me, core_stage)
            device = jnp.bitwise_xor(far, f) * core_size + jnp.bitwise_xor(core, c)
            right_ref[device] = held_refs[c][f]

    left = left_ref[...].reshape(tok_local // pack, pack, breadth, seqs)
    left = jnp.concatenate(
        [left[:, k].reshape(tok_local // pack * breadth, seqs) for k in range(pack)], axis=1
    )
    nothing = jnp.zeros((width, seqs), BF16)
    step = math.gcd(breadth, 2)
    for e in range(0, breadth, step):
        rows = []
        for k in range(e, e + step):
            right = jnp.concatenate(
                [
                    right_ref[d, k * per_device : (k + 1) * per_device, :]
                    for d in range(far_size * core_size)
                ],
                axis=0,
            )
            rows += [
                jnp.concatenate([right if j == k2 else nothing for j in range(pack)], axis=1)
                for k2 in range(pack)
            ]
        outer = lax.dot_general(
            left, jnp.concatenate(rows, axis=0), NT, preferred_element_type=F32
        ).astype(BF16)
        lanes = pack * width
        for k in range(step):
            outer_ref[:, (e + k) * breadth : (e + k + 1) * breadth, :] = outer[
                :, k * lanes : (k + 1) * lanes
            ].reshape(tok_local // pack, breadth, lanes)

    for q in range(tok_local // pack):
        projected = jnp.dot(weight_ref[...], outer_ref[q], preferred_element_type=F32)
        projected = (projected * share_ref[q : q + 1]).T
        for k in range(pack):
            i = q * pack + k
            mine = projected[k * width : (k + 1) * width]
            out_ref[i] = (base_ref[i] + mine).astype(BF16)


def pair_part(me, left, weight_t, share, base, held, stages):
    tok_local, breadth, seqs = left.shape
    pair_width = weight_t.shape[0]
    far_size, block = held[0].shape[0], held[0].shape[1:]
    width = base.shape[1]
    pack = max(1, LANES // width)
    vmem = pl.BlockSpec(memory_space=pltpu.VMEM)
    return pl.pallas_call(
        functools.partial(pair_kernel, stages),
        in_specs=[pl.BlockSpec(memory_space=pltpu.SMEM)] + [vmem] * (4 + len(held)),
        out_specs=vmem,
        scratch_shapes=[
            pltpu.VMEM((far_size * len(held), *block), BF16),
            pltpu.VMEM((tok_local // pack, breadth * breadth, pack * width), BF16),
        ],
        out_shape=jax.ShapeDtypeStruct(base.shape, BF16),
        compiler_params=pltpu.CompilerParams(vmem_limit_bytes=24 * 2**20),
        cost_estimate=pl.CostEstimate(
            flops=2 * tok_local * width * breadth * breadth * (seqs + pair_width),
            bytes_accessed=8 * tok_local * width * pair_width,
            transcendentals=0,
        ),
        name="pair_part",
    )(me, left, weight_t, share, base, *held)


def finish_kernel(stages, me_ref, back_ref, *refs):
    far_stage, near_stage, _ = stages
    near_size = near_stage[1]
    part_refs, refs = refs[:near_size], refs[near_size:]
    pair_out_ref, changed_out_ref, pair_ref, changed_ref, sems = refs
    devices, sequences = back_ref.shape[:2]
    for d in range(devices):
        for n in range(sequences):
            changed_ref[n, d] = back_ref[d, n]
    copies = [pltpu.make_async_copy(changed_ref, changed_out_ref, sems.at[0])]
    copies[0].start()
    chunk = part_refs[0].shape[1] // far_stage[1]
    near = digit(me_ref[0], near_stage)
    for n in range(near_size):
        for f in range(far_stage[1]):
            chip = f * near_size + jnp.bitwise_xor(near, n)
            here = pl.ds(pl.multiple_of(chip * chunk, chunk), chunk)
            pair_ref[:, here, :] = part_refs[n][:, f * chunk : (f + 1) * chunk, :]
    copies.append(pltpu.make_async_copy(pair_ref, pair_out_ref, sems.at[1]))
    copies[1].start()
    for copy in copies:
        copy.wait()


def finish(me, back, parts, stages):
    size, seq_local, tok_local, channels = back.shape
    rows, width, pair_width = parts[0].shape
    pair_shape = (rows, width * len(parts), pair_width)
    changed_shape = (seq_local, size, tok_local, channels)
    vmem, anywhere = pl.BlockSpec(memory_space=pltpu.VMEM), pl.BlockSpec(memory_space=pl.ANY)
    return pl.pallas_call(
        functools.partial(finish_kernel, stages),
        in_specs=[pl.BlockSpec(memory_space=pltpu.SMEM)] + [vmem] * (1 + len(parts)),
        out_specs=(anywhere, anywhere),
        scratch_shapes=[
            pltpu.VMEM(pair_shape, BF16),
            pltpu.VMEM(changed_shape, BF16),
            pltpu.SemaphoreType.DMA((2,)),
        ],
        out_shape=(
            jax.ShapeDtypeStruct(pair_shape, BF16),
            jax.ShapeDtypeStruct(changed_shape, BF16),
        ),
        compiler_params=pltpu.CompilerParams(vmem_limit_bytes=24 * 2**20),
        name="finish",
    )(me, back, *parts)


def gather_stages(size):
    chips = size // 2
    high = 2 ** math.ceil(math.log2(chips) / 2)
    low = chips // high
    return [(2 * low, high), (2, low), (1, 2)]


def exchange(held, size, distance):
    return lax.ppermute(held, "wide", [(d, d ^ distance) for d in range(size)])


def gather_column(block, size, stages):
    (far, far_size), _, (core, core_size) = stages
    block = block[None]
    column = jnp.concatenate(
        [block] + [exchange(block, size, f * far) for f in range(1, far_size)], axis=0
    )
    return [column] + [exchange(column, size, c * core) for c in range(1, core_size)]


def on_device(
    size,
    homolog_stack_state,
    present_flags,
    chain_ordinal_labels,
    pairwise_repr,
    heeding_normalizer_gains,
    retrieval_weights_qkv,
    logistic_weights,
    logistic_intercept,
    emitted_weights,
    dyadic_normalizer_gains,
    former_operand_weights,
    latter_operand_weights,
    flattened_outer_projection,
    clipped_separation_embedding,
):
    me = lax.axis_index("wide")
    seq_local, columns, channels = homolog_stack_state.shape
    tok_local = pairwise_repr.shape[0]
    seqs = seq_local * size
    breadth = former_operand_weights.shape[1]
    pair_width = flattened_outer_projection.shape[1]
    stages = gather_stages(size)

    sent = homolog_stack_state.reshape(seq_local, size, tok_local, channels).transpose(1, 0, 2, 3)
    x_rows = lax.all_to_all(sent, "wide", 0, 0, tiled=True)
    x_rows = x_rows.reshape(seqs * tok_local, channels)

    flags = present_flags.astype(F32)
    mine = lax.dynamic_slice_in_dim(flags, me * tok_local, tok_local, 1)
    flag_rows = mine.T[:, None, :]
    masks = (1000000000.0 * math.log2(math.e)) * (mine - 1.0)
    bias = jnp.pad(masks, ((0, 0), (0, LANES - tok_local))).astype(BF16)
    gains = jnp.stack([heeding_normalizer_gains, dyadic_normalizer_gains])
    weights_t = retrieval_weights_qkv.T
    wqvg = jnp.concatenate(
        [weights_t[:channels], weights_t[2 * channels :], logistic_weights.T], axis=0
    )
    wk = retrieval_weights_qkv[:, channels : 2 * channels]
    wlr = jnp.concatenate([former_operand_weights.T, latter_operand_weights.T], axis=0)
    projection_t = (
        flattened_outer_projection.reshape(breadth, breadth, pair_width)
        .transpose(2, 1, 0)
        .reshape(pair_width, breadth * breadth)
    )
    (_, far_size), (near, near_size), (_, core_size) = stages
    my_near = digit(me, stages[1])
    chunk = core_size * tok_local
    width = far_size * chunk
    pack = max(1, LANES // width)

    def near_columns(values, axis, near_digit):
        shape = values.shape
        split = values.reshape(shape[:axis] + (far_size, near_size, chunk) + shape[axis + 1 :])
        taken = lax.dynamic_index_in_dim(split, near_digit, axis + 1, keepdims=False)
        return taken.reshape(shape[:axis] + (width,) + shape[axis + 1 :])

    flags_here = near_columns(flags, 1, my_near)
    labels_here = near_columns(chain_ordinal_labels, 0, my_near)
    span = clipped_separation_embedding.shape[0]
    shares, bases = [], []
    for n in range(near_size):
        first = jnp.bitwise_xor(me, n * near) * tok_local
        rows_flags = lax.dynamic_slice_in_dim(flags, first, tok_local, 1)
        counts = jnp.dot(rows_flags.T, flags_here, precision=lax.Precision.HIGHEST)
        shares.append((1.0 / counts).reshape(tok_local // pack, pack * width))
        labels = lax.dynamic_slice_in_dim(chain_ordinal_labels, first, tok_local, 0)
        offsets = (
            jnp.clip(labels[:, None] - labels_here[None, :], -RELPOS_CLIP, RELPOS_CLIP)
            + RELPOS_CLIP
        )
        one_hot = (offsets[:, :, None] == jnp.arange(span, dtype=jnp.int32)[None, None, :]).astype(
            BF16
        )
        relpos = jnp.dot(
            one_hot.reshape(tok_local * width, span),
            clipped_separation_embedding,
            preferred_element_type=F32,
        ).reshape(tok_local, width, pair_width)
        entries = near_columns(pairwise_repr, 1, jnp.bitwise_xor(my_near, n))
        if n:
            entries = exchange(entries, size, n * near)
        bases.append(entries.astype(F32) + relpos)

    x_rows, bases, shares, projection_t = lax.optimization_barrier(
        (x_rows, bases, shares, projection_t)
    )

    changed_rows, left, right = attention(
        x_rows,
        bias,
        flag_rows,
        gains,
        wqvg,
        wk,
        logistic_intercept[:, None],
        emitted_weights,
        wlr,
        tok_local,
    )

    me = me.reshape(1)
    held = gather_column(right, size, stages)
    back = lax.all_to_all(
        changed_rows.reshape(size, seq_local, tok_local, channels), "wide", 0, 0, tiled=True
    )
    lefts = [left] + [exchange(left, size, n * near) for n in range(1, near_size)]
    parts = []
    for n in range(near_size):
        part = pair_part(me, lefts[n], projection_t, shares[n], bases[n], held, stages)
        parts.append(exchange(part, size, n * near) if n else part)
    couple_state_changed, homolog_changed = finish(me, back, parts, stages)
    return (homolog_changed.reshape(seq_local, columns, channels), couple_state_changed)


def solution(mesh):
    in_specs = (
        P(("grp", "wide"), None, None),
        P("grp", None),
        P("grp"),
        P(("grp", "wide"), None, None),
    ) + (P(),) * 10
    out_specs = (P(("grp", "wide"), None, None), P(("grp", "wide"), None, None))
    return jax.shard_map(
        functools.partial(on_device, mesh.shape["wide"]),
        mesh=mesh,
        in_specs=in_specs,
        out_specs=out_specs,
        check_vma=False,
    )
```

```python
import functools
import math

import jax
import jax.numpy as jnp
from jax import lax
from jax.experimental import pallas as pl
from jax.experimental.pallas import tpu as pltpu
from jax.sharding import PartitionSpec as P


RELPOS_CLIP = 32
HEAD_SIZE = 32
EPSILON = 1e-05
LANES = 128
F32 = jnp.float32
BF16 = jnp.bfloat16


NT = (((1,), (1,)), ((), ()))
TN = (((0,), (0,)), ((), ()))


def standardize(values, gain_row):
    mean = jnp.mean(values, axis=-1, keepdims=True)
    centered = values - mean
    variance = jnp.mean(centered * centered, axis=-1, keepdims=True)
    return centered * lax.rsqrt(variance + EPSILON) * gain_row


def put_rows(ref, rows, values):
    for part in range(ref.shape[0]):
        ref[part, rows, :] = values[:, part * LANES : (part + 1) * LANES]


def take_rows(ref, rows):
    return jnp.concatenate([ref[part, rows, :] for part in range(ref.shape[0])], axis=1)


def attention_kernel(
    tokens,
    x_ref,
    bias_ref,
    flag_ref,
    gains_ref,
    wqvg_ref,
    wk_ref,
    intercept_ref,
    wo_ref,
    wlr_ref,
    hc_ref,
    left_ref,
    right_ref,
    xf_ref,
    normed_ref,
    hcf_ref,
    rf_ref,
    queries_ref,
    keys_ref,
    values_ref,
    gate_ref,
    gated_ref,
    *group_refs,
):
    logits_refs, weights_refs = group_refs[::2], group_refs[1::2]
    rows, channels = x_ref.shape
    seqs = rows // tokens
    breadth = wlr_ref.shape[0] // 2
    group_heads = LANES // HEAD_SIZE
    scale = math.log2(math.e) / math.sqrt(HEAD_SIZE)

    values = x_ref[...].astype(F32)
    put_rows(xf_ref, slice(None), values)
    put_rows(normed_ref, slice(None), standardize(values, gains_ref[0:1, :]))

    def rows_of(ref, t):
        return take_rows(ref, pl.ds(t, seqs, stride=tokens))

    def project(first, count):
        near = range(first, first + count)
        normed = jnp.concatenate([rows_of(normed_ref, t) for t in near], axis=0).astype(BF16)
        qvg = lax.dot_general(wqvg_ref[...], normed, NT, preferred_element_type=F32)
        keys = jnp.dot(normed, wk_ref[...], preferred_element_type=F32).astype(BF16)
        gate = 0.5 * jnp.tanh(0.5 * (qvg[2 * channels :] + intercept_ref[...])) + 0.5
        for k, t in enumerate(near):
            at = slice(k * seqs, (k + 1) * seqs)
            queries_ref[t] = qvg[:channels, at].astype(BF16)
            values_ref[t] = qvg[channels : 2 * channels, at].astype(BF16)
            gate_ref[t] = gate[:, at]
            keys_ref[t] = keys[at]

    groups = channels // LANES

    def score(t, held):
        token_row = lax.broadcasted_iota(jnp.int32, (LANES, seqs), 0) == t
        token_row = jnp.where(token_row, 1.0, 0.0).astype(BF16)
        for g in range(groups):
            keys_g = jnp.concatenate(
                [keys_ref[t, :, g * LANES : (g + 1) * LANES], bias_ref[...]], axis=1
            )
            columns = []
            for h in range(group_heads):
                first = g * LANES + h * HEAD_SIZE
                parts = [queries_ref[t, first : first + HEAD_SIZE], token_row]
                above, below = h * HEAD_SIZE, LANES - (h + 1) * HEAD_SIZE
                if below:
                    parts.insert(1, jnp.zeros((below, seqs), BF16))
                if above:
                    parts.insert(0, jnp.zeros((above, seqs), BF16))
                columns.append(jnp.concatenate(parts, axis=0))
            logits_refs[held][g] = jnp.dot(
                keys_g, jnp.concatenate(columns, axis=1), preferred_element_type=F32
            )

    def weigh(held):
        for g in range(groups):
            for h in range(group_heads):
                head = slice(h * seqs, (h + 1) * seqs)
                logits = logits_refs[held][g, :, head]
                highest = jnp.max(logits, axis=0, keepdims=True)
                powers = jnp.exp2((logits - highest) * scale)
                share = 1.0 / jnp.sum(powers, axis=0, keepdims=True)
                weights_refs[held][g, :, head] = (powers * share).astype(BF16)

    def mix(t, held):
        for g in range(groups):
            for h in range(group_heads):
                head = slice(g * LANES + h * HEAD_SIZE, g * LANES + (h + 1) * HEAD_SIZE)
                mixed = jnp.dot(
                    values_ref[t, head],
                    weights_refs[held][g, :, h * seqs : (h + 1) * seqs],
                    preferred_element_type=F32,
                )
                gated_ref[t, head] = (mixed * gate_ref[t, head]).astype(BF16)

    project(0, 2)
    score(0, 0)
    for t in range(tokens):
        if t % 2 == 0 and t + 2 < tokens:
            project(t + 2, 2)
        if t > 0:
            mix(t - 1, (t - 1) % 2)
        weigh(t % 2)
        if t + 1 < tokens:
            score(t + 1, (t + 1) % 2)
    mix(tokens - 1, (tokens - 1) % 2)

    for t in range(tokens):
        delta = lax.dot_general(gated_ref[t], wo_ref[...], TN, preferred_element_type=F32)
        changed = (rows_of(xf_ref, t) + delta).astype(BF16).astype(F32)
        put_rows(hcf_ref, pl.ds(t, seqs, stride=tokens), changed)
        normed2 = standardize(changed, gains_ref[1:2, :]).astype(BF16)
        factors = lax.dot_general(wlr_ref[...], normed2, NT, preferred_element_type=F32)
        factors = factors * flag_ref[t]
        left_ref[t] = factors[:breadth].astype(BF16)
        rf_ref[pl.ds(t, breadth, stride=tokens), :] = factors[breadth:]

    hc_ref[...] = take_rows(hcf_ref, slice(None)).astype(BF16)
    right_ref[...] = rf_ref[...].astype(BF16)


def attention(x_rows, bias, flag_rows, gains, wqvg, wk, intercept, wo, wlr, tokens):
    rows, channels = x_rows.shape
    seqs = rows // tokens
    breadth = wlr.shape[0] // 2
    groups, group_heads = channels // LANES, LANES // HEAD_SIZE
    slab = pltpu.VMEM((channels // LANES, rows, LANES), F32)
    vmem = pl.BlockSpec(memory_space=pltpu.VMEM)
    return pl.pallas_call(
        functools.partial(attention_kernel, tokens),
        out_shape=(
            jax.ShapeDtypeStruct((rows, channels), BF16),
            jax.ShapeDtypeStruct((tokens, breadth, seqs), BF16),
            jax.ShapeDtypeStruct((breadth * tokens, seqs), BF16),
        ),
        in_specs=[vmem] * 9,
        out_specs=(vmem, vmem, vmem),
        scratch_shapes=[
            slab,
            slab,
            slab,
            pltpu.VMEM((breadth * tokens, seqs), F32),
            pltpu.VMEM((tokens, channels, seqs), BF16),
            pltpu.VMEM((tokens, seqs, channels), BF16),
            pltpu.VMEM((tokens, channels, seqs), BF16),
            pltpu.VMEM((tokens, channels, seqs), F32),
            pltpu.VMEM((tokens, channels, seqs), BF16),
        ]
        + [
            pltpu.VMEM((groups, seqs, group_heads * seqs), F32),
            pltpu.VMEM((groups, seqs, group_heads * seqs), BF16),
        ]
        * 2,
        compiler_params=pltpu.CompilerParams(vmem_limit_bytes=24 * 2**20),
        cost_estimate=pl.CostEstimate(
            flops=2 * rows * channels * (6 * channels),
            bytes_accessed=4 * rows * channels,
            transcendentals=0,
        ),
        name="attention",
    )(x_rows, bias, flag_rows, gains, wqvg, wk, intercept, wo, wlr)


def digit(me, stage):
    stride, members = stage
    return jnp.bitwise_and(me // stride, members - 1)


def pair_kernel(
    stages, me_ref, left_ref, weight_ref, share_ref, base_ref, *refs
):
    far_stage, _, core_stage = stages
    far_size, core_size = far_stage[1], core_stage[1]
    held_refs, (out_ref, right_ref, outer_ref) = refs[:core_size], refs[core_size:]
    tok_local, breadth, seqs = left_ref.shape
    per_device = held_refs[0].shape[1] // breadth
    width = base_ref.shape[1]
    pack = max(1, LANES // width)
    me = me_ref[0]

    for c in range(core_size):
        for f in range(far_size):
            far, core = digit(me, far_stage), digit(me, core_stage)
            device = jnp.bitwise_xor(far, f) * core_size + jnp.bitwise_xor(core, c)
            right_ref[device] = held_refs[c][f]

    left = left_ref[...].reshape(tok_local // pack, pack, breadth, seqs)
    left = jnp.concatenate(
        [left[:, k].reshape(tok_local // pack * breadth, seqs) for k in range(pack)], axis=1
    )
    nothing = jnp.zeros((width, seqs), BF16)
    step = math.gcd(breadth, 2)
    for e in range(0, breadth, step):
        rows = []
        for k in range(e, e + step):
            right = jnp.concatenate(
                [
                    right_ref[d, k * per_device : (k + 1) * per_device, :]
                    for d in range(far_size * core_size)
                ],
                axis=0,
            )
            rows += [
                jnp.concatenate([right if j == k2 else nothing for j in range(pack)], axis=1)
                for k2 in range(pack)
            ]
        outer = lax.dot_general(
            left, jnp.concatenate(rows, axis=0), NT, preferred_element_type=F32
        ).astype(BF16)
        lanes = pack * width
        for k in range(step):
            outer_ref[:, (e + k) * breadth : (e + k + 1) * breadth, :] = outer[
                :, k * lanes : (k + 1) * lanes
            ].reshape(tok_local // pack, breadth, lanes)

    for q in range(tok_local // pack):
        projected = jnp.dot(weight_ref[...], outer_ref[q], preferred_element_type=F32)
        projected = (projected * share_ref[q : q + 1]).T
        for k in range(pack):
            i = q * pack + k
            mine = projected[k * width : (k + 1) * width]
            out_ref[i] = (base_ref[i] + mine).astype(BF16)


def pair_part(me, left, weight_t, share, base, held, stages):
    tok_local, breadth, seqs = left.shape
    pair_width = weight_t.shape[0]
    far_size, block = held[0].shape[0], held[0].shape[1:]
    width = base.shape[1]
    pack = max(1, LANES // width)
    vmem = pl.BlockSpec(memory_space=pltpu.VMEM)
    return pl.pallas_call(
        functools.partial(pair_kernel, stages),
        in_specs=[pl.BlockSpec(memory_space=pltpu.SMEM)] + [vmem] * (4 + len(held)),
        out_specs=vmem,
        scratch_shapes=[
            pltpu.VMEM((far_size * len(held), *block), BF16),
            pltpu.VMEM((tok_local // pack, breadth * breadth, pack * width), BF16),
        ],
        out_shape=jax.ShapeDtypeStruct(base.shape, BF16),
        compiler_params=pltpu.CompilerParams(vmem_limit_bytes=24 * 2**20),
        cost_estimate=pl.CostEstimate(
            flops=2 * tok_local * width * breadth * breadth * (seqs + pair_width),
            bytes_accessed=8 * tok_local * width * pair_width,
            transcendentals=0,
        ),
        name="pair_part",
    )(me, left, weight_t, share, base, *held)


def finish_kernel(stages, me_ref, back_ref, *refs):
    far_stage, near_stage, _ = stages
    near_size = near_stage[1]
    part_refs, refs = refs[:near_size], refs[near_size:]
    pair_out_ref, changed_out_ref, pair_ref, changed_ref, sems = refs
    devices, sequences = back_ref.shape[:2]
    copies = []
    for n in range(sequences):
        for d in range(devices):
            changed_ref[n, d] = back_ref[d, n]
        copies.append(
            pltpu.make_async_copy(changed_ref.at[n], changed_out_ref.at[n], sems.at[n])
        )
        copies[-1].start()
    chunk = part_refs[0].shape[1] // far_stage[1]
    near = digit(me_ref[0], near_stage)
    for n in range(near_size):
        for f in range(far_stage[1]):
            chip = f * near_size + jnp.bitwise_xor(near, n)
            here = pl.ds(pl.multiple_of(chip * chunk, chunk), chunk)
            pair_ref[:, here, :] = part_refs[n][:, f * chunk : (f + 1) * chunk, :]
    copies.append(pltpu.make_async_copy(pair_ref, pair_out_ref, sems.at[sequences]))
    copies[-1].start()
    for copy in copies:
        copy.wait()


def finish(me, back, parts, stages):
    size, seq_local, tok_local, channels = back.shape
    rows, width, pair_width = parts[0].shape
    pair_shape = (rows, width * len(parts), pair_width)
    changed_shape = (seq_local, size, tok_local, channels)
    vmem, anywhere = pl.BlockSpec(memory_space=pltpu.VMEM), pl.BlockSpec(memory_space=pl.ANY)
    return pl.pallas_call(
        functools.partial(finish_kernel, stages),
        in_specs=[pl.BlockSpec(memory_space=pltpu.SMEM)] + [vmem] * (1 + len(parts)),
        out_specs=(anywhere, anywhere),
        scratch_shapes=[
            pltpu.VMEM(pair_shape, BF16),
            pltpu.VMEM(changed_shape, BF16),
            pltpu.SemaphoreType.DMA((seq_local + 1,)),
        ],
        out_shape=(
            jax.ShapeDtypeStruct(pair_shape, BF16),
            jax.ShapeDtypeStruct(changed_shape, BF16),
        ),
        compiler_params=pltpu.CompilerParams(vmem_limit_bytes=24 * 2**20),
        name="finish",
    )(me, back, *parts)


def gather_stages(size):
    chips = size // 2
    high = 2 ** math.ceil(math.log2(chips) / 2)
    low = chips // high
    return [(2 * low, high), (2, low), (1, 2)]


def exchange(held, size, distance):
    return lax.ppermute(held, "wide", [(d, d ^ distance) for d in range(size)])


def gather_column(block, size, stages):
    (far, far_size), _, (core, core_size) = stages
    block = block[None]
    column = jnp.concatenate(
        [block] + [exchange(block, size, f * far) for f in range(1, far_size)], axis=0
    )
    return [column] + [exchange(column, size, c * core) for c in range(1, core_size)]


def on_device(
    size,
    homolog_stack_state,
    present_flags,
    chain_ordinal_labels,
    pairwise_repr,
    heeding_normalizer_gains,
    retrieval_weights_qkv,
    logistic_weights,
    logistic_intercept,
    emitted_weights,
    dyadic_normalizer_gains,
    former_operand_weights,
    latter_operand_weights,
    flattened_outer_projection,
    clipped_separation_embedding,
):
    me = lax.axis_index("wide")
    seq_local, columns, channels = homolog_stack_state.shape
    tok_local = pairwise_repr.shape[0]
    seqs = seq_local * size
    breadth = former_operand_weights.shape[1]
    pair_width = flattened_outer_projection.shape[1]
    stages = gather_stages(size)

    sent = homolog_stack_state.reshape(seq_local, size, tok_local, channels).transpose(1, 0, 2, 3)
    x_rows = lax.all_to_all(sent, "wide", 0, 0, tiled=True)
    x_rows = x_rows.reshape(seqs * tok_local, channels)

    flags = present_flags.astype(F32)
    mine = lax.dynamic_slice_in_dim(flags, me * tok_local, tok_local, 1)
    flag_rows = mine.T[:, None, :]
    masks = (1000000000.0 * math.sqrt(HEAD_SIZE)) * (mine - 1.0)
    bias = jnp.pad(masks, ((0, 0), (0, LANES - tok_local))).astype(BF16)
    gains = jnp.stack([heeding_normalizer_gains, dyadic_normalizer_gains])
    weights_t = retrieval_weights_qkv.T
    wqvg = jnp.concatenate(
        [weights_t[:channels], weights_t[2 * channels :], logistic_weights.T], axis=0
    )
    wk = retrieval_weights_qkv[:, channels : 2 * channels]
    wlr = jnp.concatenate([former_operand_weights.T, latter_operand_weights.T], axis=0)
    projection_t = (
        flattened_outer_projection.reshape(breadth, breadth, pair_width)
        .transpose(2, 1, 0)
        .reshape(pair_width, breadth * breadth)
    )
    (_, far_size), (near, near_size), (_, core_size) = stages
    my_near = digit(me, stages[1])
    chunk = core_size * tok_local
    width = far_size * chunk
    pack = max(1, LANES // width)

    def near_columns(values, axis, near_digit):
        shape = values.shape
        split = values.reshape(shape[:axis] + (far_size, near_size, chunk) + shape[axis + 1 :])
        taken = lax.dynamic_index_in_dim(split, near_digit, axis + 1, keepdims=False)
        return taken.reshape(shape[:axis] + (width,) + shape[axis + 1 :])

    flags_here = near_columns(flags, 1, my_near)
    labels_here = near_columns(chain_ordinal_labels, 0, my_near)
    span = clipped_separation_embedding.shape[0]
    shares, bases = [], []
    for n in range(near_size):
        first = jnp.bitwise_xor(me, n * near) * tok_local
        rows_flags = lax.dynamic_slice_in_dim(flags, first, tok_local, 1)
        counts = jnp.dot(rows_flags.T, flags_here, precision=lax.Precision.HIGHEST)
        shares.append((1.0 / counts).reshape(tok_local // pack, pack * width))
        labels = lax.dynamic_slice_in_dim(chain_ordinal_labels, first, tok_local, 0)
        offsets = (
            jnp.clip(labels[:, None] - labels_here[None, :], -RELPOS_CLIP, RELPOS_CLIP)
            + RELPOS_CLIP
        )
        one_hot = (offsets[:, :, None] == jnp.arange(span, dtype=jnp.int32)[None, None, :]).astype(
            BF16
        )
        relpos = jnp.dot(
            one_hot.reshape(tok_local * width, span),
            clipped_separation_embedding,
            preferred_element_type=F32,
        ).reshape(tok_local, width, pair_width)
        entries = near_columns(pairwise_repr, 1, jnp.bitwise_xor(my_near, n))
        if n:
            entries = exchange(entries, size, n * near)
        bases.append(entries.astype(F32) + relpos)

    x_rows, bases, shares, projection_t = lax.optimization_barrier(
        (x_rows, bases, shares, projection_t)
    )

    changed_rows, left, right = attention(
        x_rows,
        bias,
        flag_rows,
        gains,
        wqvg,
        wk,
        logistic_intercept[:, None],
        emitted_weights,
        wlr,
        tok_local,
    )

    me = me.reshape(1)
    held = gather_column(right, size, stages)
    back = lax.all_to_all(
        changed_rows.reshape(size, seq_local, tok_local, channels), "wide", 0, 0, tiled=True
    )
    lefts = [left] + [exchange(left, size, n * near) for n in range(1, near_size)]
    parts = []
    for n in range(near_size):
        part = pair_part(me, lefts[n], projection_t, shares[n], bases[n], held, stages)
        parts.append(exchange(part, size, n * near) if n else part)
    couple_state_changed, homolog_changed = finish(me, back, parts, stages)
    return (homolog_changed.reshape(seq_local, columns, channels), couple_state_changed)


def solution(mesh):
    in_specs = (
        P(("grp", "wide"), None, None),
        P("grp", None),
        P("grp"),
        P(("grp", "wide"), None, None),
    ) + (P(),) * 10
    out_specs = (P(("grp", "wide"), None, None), P(("grp", "wide"), None, None))
    return jax.shard_map(
        functools.partial(on_device, mesh.shape["wide"]),
        mesh=mesh,
        in_specs=in_specs,
        out_specs=out_specs,
        check_vma=False,
    )
```
